128 devices in a mesh: tp: 4 (over z_lo, core), worker: 32 (over z_hi, y, x).
Axes of the slice: x: 4, y: 4, z: 4 (z_hi: 2, z_lo: 2; z = z_hi * 2 + z_lo), core: 2. Of those that a mesh axis runs over, the one named last changes fastest.
Arguments:
- queries: bfloat16 [12288, 2560], P('worker', 'tp'), may hold values from -6 to 6
- keys: bfloat16 [12288, 2560], P('worker', 'tp'), may hold values from -6 to 6
- values: bfloat16 [12288, 2560], P('worker', 'tp'), may hold values from -32 to 32
- out_grad: bfloat16 [12288, 5120], P('worker', 'tp'), may hold values from -24 to 24
- segments: int32 [12288], P('worker'), may hold values from 0 to 3, as said below
- drift: bfloat16 [32, 2560, 5120], P('worker', 'tp'), may hold values from -3 to 3
- master: float32 [2560, 5120], P(('tp', 'worker')), may hold values from -4 to 4
- momentum: float32 [2560, 5120], P(('tp', 'worker')), may hold values from -1.5 to 1.5
Outputs:
- new_params: bfloat16 [2560, 5120], P('tp')
- new_master: float32 [2560, 5120], P(('tp', 'worker'))
- new_momentum: float32 [2560, 5120], P(('tp', 'worker'))
The draws below stay inside these ranges and needn't reach their ends.
Inputs may be any that keep to these rules, and one draw needn't show every extreme that they name: `segments`: within each worker's 384 tokens the document id starts at 0, never falls and ends at 3.
All inputs are finite; a program needn't handle non-finite values.
Results may differ from the reference program's by a relative error of at most 0.0065.
Values may be sent and summed in bfloat16 or wider, within the bound.
No kernel may reach another device: no remote copies, remote signals or barrier semaphores. Data moves between devices by JAX's collectives and lax.ppermute only.
A program may use at most 128 MiB of HBM per device.

```python
import math
import jax
import jax.numpy as jnp
from jax import lax

D = 5120
HEADS = 20
HD = 128
TOK_W = 384
DOCS = 4
WORKERS = 32
TOKENS = 12288
ROWS = 2560


def draw_queries(key, part):
    drawn = jnp.clip(jax.random.normal(jax.random.fold_in(key, 1), (TOKENS, HEADS * HD), jnp.float32), -5.0, 5.0)
    return drawn.astype(jnp.bfloat16)


def draw_keys(key, part):
    drawn = jnp.clip(jax.random.normal(jax.random.fold_in(key, 2), (TOKENS, HEADS * HD), jnp.float32), -5.0, 5.0)
    return drawn.astype(jnp.bfloat16)


def draw_values(key, part):
    channel = jnp.arange(HEADS * HD, dtype=jnp.int32).reshape(1, HEADS * HD)
    head_float = (channel // HD).astype(jnp.float32)
    rise = jnp.sqrt(1.0 + 4.0 * head_float / max(HEADS - 1, 1))
    spread = jnp.exp(0.5 * math.log(10.0) * jax.random.uniform(jax.random.fold_in(key, 3), (1, HEADS * HD), jnp.float32))
    drawn = jnp.clip(jax.random.normal(jax.random.fold_in(key, 8), (TOKENS, HEADS * HD), jnp.float32), -4.0, 4.0)
    return (drawn * rise * spread).astype(jnp.bfloat16)


def draw_out_grad(key, part):
    spread = jnp.exp(0.5 * math.log(10.0) * jax.random.uniform(jax.random.fold_in(key, 5), (1, D), jnp.float32))
    drawn = jnp.clip(jax.random.normal(jax.random.fold_in(key, 4), (TOKENS, D), jnp.float32), -4.0, 4.0)
    return (drawn * spread).astype(jnp.bfloat16)


def draw_segments(key, part):
    worker_count = TOKENS // TOK_W
    spacing = TOK_W // DOCS
    reach = spacing // 4
    offsets = jax.random.randint(key, (worker_count, DOCS - 1), -reach, reach + 1)
    bounds = (jnp.arange(1, DOCS, dtype=jnp.int32) * spacing).reshape(1, DOCS - 1) + offsets
    place = jnp.arange(TOK_W, dtype=jnp.int32).reshape(1, TOK_W, 1)
    ids = jnp.sum((place >= bounds[:, None, :]).astype(jnp.int32), axis=2)
    return ids.reshape(TOKENS).astype(jnp.int32)


def spiked(entries, rng, source, target, shards_of, factor):
    def block_of(dim):
        return (jnp.arange(entries.shape[dim]) // (entries.shape[dim] // shards_of)).reshape((-1,) + (1,) * (entries.ndim - 1 - dim))

    one_side = jax.random.permutation(rng, shards_of)[block_of(target)]
    second = (block_of(target) + shards_of // 2) % shards_of
    return jnp.where((block_of(source) == one_side) | (block_of(source) == second), factor * entries, entries)


def block_scale(own_key, shape, cuts, smallest, largest):
    def one(dim, parts):
        draws = jax.random.uniform(jax.random.fold_in(jax.random.fold_in(own_key, 6), dim), (parts,), jnp.float32, smallest / len(cuts), largest / len(cuts))
        return jnp.repeat(jnp.exp(draws), shape[dim] // parts).reshape((-1,) + (1,) * (len(shape) - dim - 1))

    gain = one(*cuts[0])
    for cut in cuts[1:]:
        gain = gain * one(*cut)
    return gain


def noise(stream_key, extent, scale, bound, shards=(), kind=jnp.bfloat16):
    values = jax.random.normal(stream_key, extent, jnp.float32) * scale
    if len(shards) > 0:
        values = block_scale(stream_key, extent, shards, -0.22, 0.18) * values
    return jnp.clip(values, min=-bound, max=bound).astype(kind)


def noise_with(own_key, shape, deviation, most, split, heavy, kind=jnp.bfloat16):
    entries = deviation * jax.random.normal(own_key, shape, jnp.float32)
    if split:
        entries = entries * block_scale(own_key, shape, split, -0.22, 0.18)
    return jnp.clip(spiked(entries, jax.random.fold_in(own_key, 3), *heavy), -most, most).astype(kind)


def setup_inputs(seed: int = 0) -> dict:
    seeds = jax.random.split(jax.random.key(seed), 9)
    return {
        "queries": draw_queries(jax.random.fold_in(seeds[8], 71), 0),
        "keys": draw_keys(jax.random.fold_in(seeds[8], 71), 0),
        "values": draw_values(jax.random.fold_in(seeds[8], 71), 0),
        "out_grad": draw_out_grad(jax.random.fold_in(seeds[8], 71), 0),
        "segments": draw_segments(jax.random.fold_in(seeds[8], 71), 0),
        "drift": noise_with(seeds[5], (WORKERS, ROWS, D), 0.5, 3.0, ((0, 32), (1, 4)), (0, 1, 32, 2.75)),
        "master": noise(seeds[6], (ROWS, D), 1.0, 4.0, ((0, 128),), jnp.float32),
        "momentum": noise(seeds[7], (ROWS, D), 0.3, 1.5, ((0, 128),), jnp.float32),
    }


inner_rate = 0.8
outer_rate = 0.7
outer_mu = 0.9
neg_big = -1e+30

def head_context(query_head, key_head, value_head, allowed):
    scores = jnp.dot(query_head, key_head.T, preferred_element_type=jnp.float32) * (1.0 / math.sqrt(HD))
    scores = jnp.where(allowed, scores, neg_big)
    row_max = lax.optimization_barrier(jnp.max(scores, axis=1, keepdims=True))
    exp_scores = jnp.exp(scores - row_max)
    weights = (exp_scores / lax.optimization_barrier(jnp.sum(exp_scores, axis=1, keepdims=True))).astype(jnp.bfloat16)
    return jnp.dot(weights, value_head, preferred_element_type=jnp.float32).astype(jnp.bfloat16)

def worker_update(query_rows, key_rows, value_rows, grad_rows, segment_rows):
    position = jnp.arange(TOK_W, dtype=jnp.int32)
    allowed = (position[None, :] <= position[:, None]) & (segment_rows[None, :] == segment_rows[:, None])

    def one_head(head_index):
        first = (head_index * HD).astype(jnp.int32)
        return head_context(lax.dynamic_slice_in_dim(query_rows, first, HD, 1), lax.dynamic_slice_in_dim(key_rows, first, HD, 1), lax.dynamic_slice_in_dim(value_rows, first, HD, 1), allowed)
    context = lax.map(one_head, jnp.arange(HEADS, dtype=jnp.int32))
    gradient = jnp.einsum('htd,tc->hdc', context.astype(jnp.float32), grad_rows.astype(jnp.float32)).reshape(ROWS, D)
    rms_value = jnp.sqrt(jnp.mean(gradient * gradient) + 1e-06)
    return (inner_rate * gradient / rms_value).astype(jnp.bfloat16)

def reference(queries, keys, values, out_grad, segments, drift, master, momentum):

    def add_worker(summed, worker_index):
        first = (worker_index * TOK_W).astype(jnp.int32)

        def rows_of(array):
            return lax.dynamic_slice_in_dim(array, first, TOK_W, 0)
        update = worker_update(rows_of(queries), rows_of(keys), rows_of(values), rows_of(out_grad), rows_of(segments))
        own_drift = lax.dynamic_index_in_dim(drift, worker_index, 0, keepdims=False)
        worker_term = own_drift.astype(jnp.float32) + update.astype(jnp.float32)
        return (summed + worker_term, None)
    summed, _ = lax.scan(add_worker, jnp.zeros((ROWS, D), jnp.float32), jnp.arange(WORKERS, dtype=jnp.int32))
    mean_delta = summed / WORKERS
    new_momentum = outer_mu * momentum + mean_delta
    new_master = master - outer_rate * (mean_delta + outer_mu * new_momentum)
    return (new_master.astype(jnp.bfloat16), new_master, new_momentum)
```

```python
import math

import jax
import jax.numpy as jnp
from jax import lax
from jax.experimental import pallas as pl
from jax.experimental.pallas import tpu as pltpu
from jax.sharding import PartitionSpec as P

HD = 128
NX, NY, NZ = 4, 4, 2
TILE_R = 80
HALF_C = 640

inner_rate = 0.8
outer_rate = 0.7
outer_mu = 0.9
neg_big = -1e30
bf16 = jnp.bfloat16
f32 = jnp.float32
VMEM_LIMIT = 60 << 20


def worker_of(zh, y, x):
    return (zh % NZ) * NX * NY + (y % NY) * NX + (x % NX)


def move(value, axis, step):
    pairs = []
    for zh in range(NZ):
        for y in range(NY):
            for x in range(NX):
                to = {
                    "x": worker_of(zh, y, x + step),
                    "y": worker_of(zh, y + step, x),
                    "z": worker_of(zh + step, y, x),
                }[axis]
                pairs.append((worker_of(zh, y, x), to))
    return lax.ppermute(value, "worker", pairs)


def swap_tp(value, bit):
    return lax.ppermute(value, "tp", [(t, t ^ bit) for t in range(4)])


def attention_body(q_ref, k_ref, v_ref, seg_row_ref, seg_col_ref, ct_ref, gram_ref):
    tokens, width = q_ref.shape
    scale = 1.0 / math.sqrt(HD)
    blocks = tokens // HD
    for h in range(width // HD):
        cols = slice(h * HD, (h + 1) * HD)
        for b in range(blocks):
            queries = slice(b * HD, (b + 1) * HD)
            seen = (b + 1) * HD
            scores = lax.dot_general(
                k_ref[:seen, cols], q_ref[queries, cols], (((1,), (1,)), ((), ())),
                preferred_element_type=f32,
            ) * scale
            key_at = lax.broadcasted_iota(jnp.int32, (seen, HD), 0)
            query_at = lax.broadcasted_iota(jnp.int32, (seen, HD), 1) + b * HD
            allowed = (key_at <= query_at) & (seg_col_ref[:seen, :] == seg_row_ref[:, queries])
            scores = jnp.where(allowed, scores, neg_big)
            exp_scores = jnp.exp(scores - jnp.max(scores, axis=0, keepdims=True))
            total = jnp.sum(exp_scores, axis=0, keepdims=True)
            weights = (exp_scores * (1.0 / total)).astype(bf16)
            ct_ref[cols, queries] = lax.dot_general(
                v_ref[:seen, cols], weights, (((0,), (0,)), ((), ())),
                preferred_element_type=f32,
            ).astype(bf16)
    gram_ref[...] = lax.dot_general(
        ct_ref[...], ct_ref[...], (((0,), (0,)), ((), ())), preferred_element_type=f32
    )


def attention(queries, keys, values, segments):
    tokens, width = queries.shape
    return pl.pallas_call(
        attention_body,
        out_shape=(
            jax.ShapeDtypeStruct((width, tokens), bf16),
            jax.ShapeDtypeStruct((tokens, tokens), f32),
        ),
        compiler_params=pltpu.CompilerParams(vmem_limit_bytes=VMEM_LIMIT),
        name="attention",
    )(queries, keys, values, segments.reshape(1, tokens), segments.reshape(tokens, 1))


def column_of(tp, half, quarter):
    first = (tp ^ (2 * half) ^ (quarter // 2)) * (2 * HALF_C) + (quarter % 2) * HALF_C
    return pl.multiple_of(first, HALF_C)


def row_of(zh, y, j, ky):
    return pl.multiple_of((zh ^ j) * (NY * TILE_R) + ((y + ky) % NY) * TILE_R, TILE_R)


SEND_ORDER = (2, 1, 3, 0)


def pseudo_body(at_ref, scale_ref, ct_ref, g0_ref, g1_ref, g2_ref, g3_ref, drift_ref, *rest):
    outs, (drift_buf, rows_buf, sems) = rest[:14], rest[14:]
    x, y, zh, tp = at_ref[0], at_ref[1], at_ref[2], at_ref[3]
    scale = scale_ref[0]
    a_out, b_out = outs[:7], outs[7:]

    def copy(slot, k, half):
        return pltpu.make_async_copy(
            drift_ref.at[0, :, pl.ds(column_of(tp, half, (x + k) % NX), HALF_C)],
            drift_buf.at[slot], sems.at[slot],
        )

    steps = [(k, half) for k in SEND_ORDER for half in range(2)]
    for slot, (k, half) in enumerate(steps):
        copy(slot, k, half).start()
    for j in range(2):
        for ky in range(NY):
            first = (j * NY + ky) * TILE_R
            rows_buf[first:first + TILE_R, :] = ct_ref[pl.ds(row_of(zh, y, j, ky), TILE_R), :]

    def store(group, block, index, half, value):
        cols = slice(half * HALF_C, (half + 1) * HALF_C)
        if block == 0:
            group[0][index, :, cols] = value
        else:
            group[1 + 2 * (block - 1) + index // 2][index % 2, :, cols] = value

    for slot, (k, half) in enumerate(steps):
        quarter = (x + k) % NX
        cols = pl.ds(pl.multiple_of((quarter % 2) * HALF_C, HALF_C), HALF_C)
        near, far = (g0_ref, g1_ref) if half == 0 else (g2_ref, g3_ref)
        piece = jnp.where(quarter >= 2, far[:, cols], near[:, cols])
        copy(slot, k, half).wait()
        for j in range(2):
            rows = slice(j * NY * TILE_R, (j + 1) * NY * TILE_R)
            block = jnp.dot(rows_buf[rows, :], piece, preferred_element_type=f32)
            for ky in range(NY):
                own = drift_buf[slot, pl.ds(row_of(zh, y, j, ky), TILE_R), :]
                value = block[ky * TILE_R:(ky + 1) * TILE_R] * scale + own.astype(f32)
                value = value.astype(bf16)
                if j == 0:
                    store(a_out, k, ky, half, value)
                else:
                    store(b_out, ky, k, half, value)


def pseudo_gradient(at, scale, ct, pieces, drift):
    whole = jax.ShapeDtypeStruct((4, TILE_R, 2 * HALF_C), bf16)
    part = jax.ShapeDtypeStruct((2, TILE_R, 2 * HALF_C), bf16)
    vmem = pl.BlockSpec(memory_space=pltpu.VMEM)
    smem = pl.BlockSpec(memory_space=pltpu.SMEM)
    return pl.pallas_call(
        pseudo_body,
        out_shape=((whole,) + (part,) * 6) * 2,
        in_specs=[smem, smem] + [vmem] * 5 + [pl.BlockSpec(memory_space=pl.ANY)],
        out_specs=(vmem,) * 14,
        scratch_shapes=[
            pltpu.VMEM((8, 2 * NY * TILE_R, HALF_C), bf16),
            pltpu.VMEM(ct.shape, bf16),
            pltpu.SemaphoreType.DMA((8,)),
        ],
        compiler_params=pltpu.CompilerParams(vmem_limit_bytes=VMEM_LIMIT),
        name="pseudo_gradient",
    )(at, scale, ct, *pieces, drift)


def base_body(at_ref, master_ref, momentum_ref, base_ref):
    tp = at_ref[3]
    for quarter in range(NX):
        for half in range(2):
            cols = pl.ds(column_of(tp, half, quarter), HALF_C)
            base_ref[quarter, :, half * HALF_C:(half + 1) * HALF_C] = (
                master_ref[:, cols] - (outer_rate * outer_mu * outer_mu) * momentum_ref[:, cols]
            )


def base_rows(at, master, momentum):
    vmem = pl.BlockSpec(memory_space=pltpu.VMEM)
    return pl.pallas_call(
        base_body,
        out_shape=jax.ShapeDtypeStruct((NX, master.shape[0], 2 * HALF_C), f32),
        in_specs=[pl.BlockSpec(memory_space=pltpu.SMEM), vmem, vmem],
        out_specs=vmem,
        name="base_rows",
    )(at, master, momentum)


def outer_body(at_ref, master_ref, momentum_ref, mean_ref, new_master_ref, new_momentum_ref):
    x, tp = at_ref[0], at_ref[3]
    for quarter in range(NX):
        for half in range(2):
            cols = pl.ds(column_of(tp, half, quarter), HALF_C)
            mean = mean_ref[(quarter - x + NX) % NX, :, half * HALF_C:(half + 1) * HALF_C]
            new = outer_mu * momentum_ref[:, cols] + mean
            new_momentum_ref[:, cols] = new
            new_master_ref[:, cols] = master_ref[:, cols] - outer_rate * (mean + outer_mu * new)


def outer_rows(at, master, momentum, mean):
    vmem = pl.BlockSpec(memory_space=pltpu.VMEM)
    out = jax.ShapeDtypeStruct(master.shape, f32)
    return pl.pallas_call(
        outer_body,
        out_shape=(out, out),
        in_specs=[pl.BlockSpec(memory_space=pltpu.SMEM), vmem, vmem, vmem],
        out_specs=(vmem, vmem),
        name="outer_rows",
    )(at, master, momentum, mean)


def place_body(at_ref, *rest):
    tiles, out_ref, sems = rest[:-2], rest[-2], rest[-1]
    x, y, zh, tp = at_ref[0], at_ref[1], at_ref[2], at_ref[3]
    copies = []
    for n, (where, (j, ky, kx)) in enumerate(TILES):
        ref, index = where
        for half in range(2):
            cols = slice(half * HALF_C, (half + 1) * HALF_C)
            source = tiles[ref].at[:, cols] if index is None else tiles[ref].at[index, :, cols]
            copies.append(pltpu.make_async_copy(
                source,
                out_ref.at[pl.ds(row_of(zh, y, j, ky), TILE_R),
                           pl.ds(column_of(tp, half, (x + kx) % NX), HALF_C)],
                sems.at[2 * n + half],
            ))
    for one in copies:
        one.start()
    for one in copies:
        one.wait()


def tile_list():
    found = []
    for j in range(2):
        base = 10 * j
        for small in range(4):
            found.append(((base + small, None), (j, small, 0) if j == 0 else (j, 0, small)))
        for large in range(1, 4):
            for small in range(4):
                operand = base + 4 + 2 * (large - 1) + small // 2
                place = (j, small, large) if j == 0 else (j, large, small)
                found.append(((operand, small % 2), place))
    return found


TILES = tile_list()


def place(at, tiles, rows, width):
    hbm = pl.BlockSpec(memory_space=pl.ANY)
    return pl.pallas_call(
        place_body,
        out_shape=jax.ShapeDtypeStruct((rows, width), bf16),
        in_specs=[pl.BlockSpec(memory_space=pltpu.SMEM)] + [hbm] * len(tiles),
        out_specs=hbm,
        scratch_shapes=[pltpu.SemaphoreType.DMA((2 * len(TILES),))],
        name="place",
    )(at, *tiles)


def add(*terms):
    total = terms[0].astype(f32)
    for term in terms[1:]:
        total = total + term.astype(f32)
    return total


def reduce_route(blocks, first, second):
    own, one_a, one_b, two_a, two_b, three_a, three_b = blocks
    via_a = move(two_a, first, 1)
    via_b = move(two_b, first, -1)
    got_1b = move(one_b, first, 1)
    got_3a = move(three_a, first, -1)
    got_1a = move(add(one_a, via_a).astype(bf16), first, 1)
    got_3b = move(add(three_b, via_b).astype(bf16), first, -1)
    tiles = []
    for k in range(4):
        up, down = (got_1a, got_3a) if k < 2 else (got_1b, got_3b)
        tiles.append(add(own[k], up[k % 2], down[k % 2]))
    two = move(tiles[2].astype(bf16), second, 2)
    one = move(tiles[1].astype(bf16), second, 1)
    three = move(tiles[3].astype(bf16), second, -1)
    return add(tiles[0], one, three, two)


def gather_route(tile, first, second):
    one = move(tile, first, -1)
    three = move(tile, first, 1)
    two = move(tile, first, -2)
    half_a = jnp.stack([tile, one])
    half_b = jnp.stack([two, three])
    a1 = move(half_a, second, -1)
    b3 = move(half_b, second, 1)
    b1 = move(half_b, second, -1)
    a3 = move(half_a, second, 1)
    a2 = move(a1, second, -1)
    b2 = move(b3, second, 1)
    return [tile, one, two, three, a1, b1, a2, b2, a3, b3]


def per_device(queries, keys, values, out_grad, segments, drift, master, momentum):
    tp = lax.axis_index("tp")
    worker = lax.axis_index("worker")
    x, y, zh = worker % NX, (worker // NX) % NY, worker // (NX * NY)
    at = jnp.stack([x, y, zh, tp]).astype(jnp.int32)
    tokens = queries.shape[0]
    entries = queries.shape[1] * lax.axis_size("tp") * drift.shape[2]

    gram = lax.dot_general(out_grad, out_grad, (((1,), (1,)), ((), ())), preferred_element_type=f32)
    side = (tp % 2) * (tokens // 2)
    other = (tokens // 2) - side
    mine = lax.dynamic_slice_in_dim(gram, side, tokens // 2, 0)
    mine = mine + swap_tp(lax.dynamic_slice_in_dim(gram, other, tokens // 2, 0), 1)
    mine = mine + swap_tp(mine, 2)
    theirs = swap_tp(mine, 1)

    partner = swap_tp(out_grad, 1)
    across = swap_tp(out_grad, 2)
    across_partner = swap_tp(across, 1)

    base = base_rows(at, master, momentum)
    base_got = jnp.stack(
        [lax.dynamic_index_in_dim(base, x, 0, False)]
        + [move(lax.dynamic_index_in_dim(base, (x + k) % NX, 0, False), "x", k) for k in (1, 2, 3)]
    )
    base_tile = jnp.concatenate(
        [lax.dynamic_index_in_dim(base_got, (x - g + NX) % NX, 0, False) for g in range(NX)], axis=0
    )

    ct, own_gram = attention(queries, keys, values, segments)
    squares = jnp.sum(lax.dynamic_slice_in_dim(own_gram, side, tokens // 2, 0) * mine)
    squares = squares + jnp.sum(lax.dynamic_slice_in_dim(own_gram, other, tokens // 2, 0) * theirs)
    squares = lax.psum(squares, "tp")
    scale = (inner_rate / jnp.sqrt(squares / entries + 1e-06)).reshape(1)

    sends = pseudo_gradient(at, scale, ct, (out_grad, partner, across, across_partner), drift)
    here = reduce_route(sends[:7], "x", "y")
    there = reduce_route(sends[7:], "y", "x")
    summed = add(here, move(there.astype(bf16), "z", 1))
    mean = summed / lax.axis_size("worker")

    tile = (base_tile - (outer_rate * (1.0 + outer_mu)) * mean).astype(bf16)
    opposite = move(tile, "z", 1)
    tiles = gather_route(tile, "y", "x") + gather_route(opposite, "x", "y")

    def rows_for(k):
        return lax.dynamic_slice_in_dim(mean, ((x + k) % NX) * master.shape[0], master.shape[0], 0)

    means = jnp.stack([rows_for(0)] + [move(rows_for(NX - k), "x", -k) for k in (1, 2, 3)])
    new_master, new_momentum = outer_rows(at, master, momentum, means)
    new_params = place(at, tiles, drift.shape[1], drift.shape[2])
    return (new_params, new_master, new_momentum)


def solution(mesh):
    placed = (
        P("worker", "tp"),
        P("worker", "tp"),
        P("worker", "tp"),
        P("worker", "tp"),
        P("worker"),
        P("worker", "tp", None),
        P(("tp", "worker"), None),
        P(("tp", "worker"), None),
    )
    return jax.shard_map(
        per_device,
        mesh=mesh,
        in_specs=placed,
        out_specs=(P("tp", None), P(("tp", "worker"), None), P(("tp", "worker"), None)),
        check_vma=False,
    )
```

```python
import math

import jax
import jax.numpy as jnp
from jax import lax
from jax.experimental import pallas as pl
from jax.experimental.pallas import tpu as pltpu
from jax.sharding import PartitionSpec as P

HD = 128
NX, NY, NZ = 4, 4, 2
TILE_R = 80
HALF_C = 640

inner_rate = 0.8
outer_rate = 0.7
outer_mu = 0.9
neg_big = -1e30
bf16 = jnp.bfloat16
f32 = jnp.float32
VMEM_LIMIT = 60 << 20


def worker_of(zh, y, x):
    return (zh % NZ) * NX * NY + (y % NY) * NX + (x % NX)


def move(value, axis, step):
    pairs = []
    for zh in range(NZ):
        for y in range(NY):
            for x in range(NX):
                to = {
                    "x": worker_of(zh, y, x + step),
                    "y": worker_of(zh, y + step, x),
                    "z": worker_of(zh + step, y, x),
                }[axis]
                pairs.append((worker_of(zh, y, x), to))
    return lax.ppermute(value, "worker", pairs)


def swap_tp(value, bit):
    return lax.ppermute(value, "tp", [(t, t ^ bit) for t in range(4)])


def attention_body(q_ref, k_ref, v_ref, seg_row_ref, seg_col_ref, ct_ref, gram_ref):
    tokens, width = q_ref.shape
    scale = 1.0 / math.sqrt(HD)
    blocks = tokens // HD
    for h in range(width // HD):
        cols = slice(h * HD, (h + 1) * HD)
        for b in range(blocks):
            queries = slice(b * HD, (b + 1) * HD)
            seen = (b + 1) * HD
            scores = lax.dot_general(
                k_ref[:seen, cols], q_ref[queries, cols], (((1,), (1,)), ((), ())),
                preferred_element_type=f32,
            ) * scale
            key_at = lax.broadcasted_iota(jnp.int32, (seen, HD), 0)
            query_at = lax.broadcasted_iota(jnp.int32, (seen, HD), 1) + b * HD
            allowed = (key_at <= query_at) & (seg_col_ref[:seen, :] == seg_row_ref[:, queries])
            scores = jnp.where(allowed, scores, neg_big)
            exp_scores = jnp.exp(scores - jnp.max(scores, axis=0, keepdims=True))
            total = jnp.sum(exp_scores, axis=0, keepdims=True)
            weights = (exp_scores * (1.0 / total)).astype(bf16)
            ct_ref[cols, queries] = lax.dot_general(
                v_ref[:seen, cols], weights, (((0,), (0,)), ((), ())),
                preferred_element_type=f32,
            ).astype(bf16)
    gram_ref[...] = lax.dot_general(
        ct_ref[...], ct_ref[...], (((0,), (0,)), ((), ())), preferred_element_type=f32
    )


def attention(queries, keys, values, segments):
    tokens, width = queries.shape
    return pl.pallas_call(
        attention_body,
        out_shape=(
            jax.ShapeDtypeStruct((width, tokens), bf16),
            jax.ShapeDtypeStruct((tokens, tokens), f32),
        ),
        compiler_params=pltpu.CompilerParams(vmem_limit_bytes=VMEM_LIMIT),
        cost_estimate=pl.CostEstimate(
            flops=4_000_000_000, bytes_accessed=2_600_000, transcendentals=500_000
        ),
        name="attention",
    )(queries, keys, values, segments.reshape(1, tokens), segments.reshape(tokens, 1))


def column_of(tp, half, quarter):
    first = (tp ^ (2 * half) ^ (quarter // 2)) * (2 * HALF_C) + (quarter % 2) * HALF_C
    return pl.multiple_of(first, HALF_C)


def row_of(zh, y, j, ky):
    return pl.multiple_of((zh ^ j) * (NY * TILE_R) + ((y + ky) % NY) * TILE_R, TILE_R)


SEND_ORDER = (2, 1, 3, 0)


def pseudo_body(at_ref, scale_ref, ct_ref, g0_ref, g1_ref, g2_ref, g3_ref, drift_ref, *rest):
    outs, (drift_buf, g_buf, rows_buf, out_buf, drift_sems, g_sems, out_sems) = rest[:8], rest[8:]
    x, y, zh, tp = at_ref[0], at_ref[1], at_ref[2], at_ref[3]
    scale = scale_ref[0]
    steps = [(k, half) for k in SEND_ORDER for half in range(2)]

    def drift_copy(slot):
        k, half = steps[slot]
        return pltpu.make_async_copy(
            drift_ref.at[0, :, pl.ds(column_of(tp, half, (x + k) % NX), HALF_C)],
            drift_buf.at[slot], drift_sems.at[slot],
        )

    def g_copy(slot, ref):
        quarter = (x + steps[slot][0]) % NX
        return pltpu.make_async_copy(
            ref.at[:, pl.ds(pl.multiple_of((quarter % 2) * HALF_C, HALF_C), HALF_C)],
            g_buf.at[slot], g_sems.at[slot],
        )

    for slot, (k, half) in enumerate(steps):
        near, far = (g0_ref, g1_ref) if half == 0 else (g2_ref, g3_ref)
        quarter = (x + k) % NX
        pl.when(quarter < 2)(lambda slot=slot, near=near: g_copy(slot, near).start())
        pl.when(quarter >= 2)(lambda slot=slot, far=far: g_copy(slot, far).start())
        drift_copy(slot).start()
    for j in range(2):
        for ky in range(NY):
            first = (j * NY + ky) * TILE_R
            rows_buf[first:first + TILE_R, :] = ct_ref[pl.ds(row_of(zh, y, j, ky), TILE_R), :]

    copies = []
    for slot, (k, half) in enumerate(steps):
        cols = slice(half * HALF_C, (half + 1) * HALF_C)
        g_copy(slot, g0_ref).wait()
        drift_copy(slot).wait()
        for j in range(2):
            rows = slice(j * NY * TILE_R, (j + 1) * NY * TILE_R)
            block = jnp.dot(rows_buf[rows, :], g_buf[slot], preferred_element_type=f32)
            for ky in range(NY):
                own = drift_buf[slot, pl.ds(row_of(zh, y, j, ky), TILE_R), :]
                value = block[ky * TILE_R:(ky + 1) * TILE_R] * scale + own.astype(f32)
                group, index = (k, ky) if j == 0 else (4 + ky, k)
                out_buf[group, index, :, cols] = value.astype(bf16)
        if half == 1:
            made = [(k, None)] + [(4 + ky, k) for ky in range(NY)]
            for group, index in made:
                src, dst = out_buf.at[group], outs[group]
                if index is not None:
                    src, dst = src.at[index], dst.at[index]
                copies.append(pltpu.make_async_copy(src, dst, out_sems.at[len(copies)]))
                copies[-1].start()
    for one in copies:
        one.wait()


def pseudo_gradient(at, scale, ct, pieces, drift):
    block = jax.ShapeDtypeStruct((4, TILE_R, 2 * HALF_C), bf16)
    smem = pl.BlockSpec(memory_space=pltpu.SMEM)
    hbm = pl.BlockSpec(memory_space=pl.ANY)
    tokens, rows = ct.shape[1], ct.shape[0]
    return pl.pallas_call(
        pseudo_body,
        out_shape=(block,) * 8,
        in_specs=[smem, smem, pl.BlockSpec(memory_space=pltpu.VMEM)] + [hbm] * 5,
        out_specs=(hbm,) * 8,
        scratch_shapes=[
            pltpu.VMEM((8, rows, HALF_C), bf16),
            pltpu.VMEM((8, tokens, HALF_C), bf16),
            pltpu.VMEM(ct.shape, bf16),
            pltpu.VMEM((8, 4, TILE_R, 2 * HALF_C), bf16),
            pltpu.SemaphoreType.DMA((8,)),
            pltpu.SemaphoreType.DMA((8,)),
            pltpu.SemaphoreType.DMA((20,)),
        ],
        compiler_params=pltpu.CompilerParams(vmem_limit_bytes=VMEM_LIMIT),
        cost_estimate=pl.CostEstimate(
            flops=2 * rows * tokens * 5120, bytes_accessed=18_000_000, transcendentals=0
        ),
        name="pseudo_gradient",
    )(at, scale, ct, *pieces, drift)


def base_body(at_ref, master_ref, momentum_ref, base_ref):
    tp = at_ref[3]
    for quarter in range(NX):
        for half in range(2):
            cols = pl.ds(column_of(tp, half, quarter), HALF_C)
            base_ref[quarter, :, half * HALF_C:(half + 1) * HALF_C] = (
                master_ref[:, cols] - (outer_rate * outer_mu * outer_mu) * momentum_ref[:, cols]
            )


def base_rows(at, master, momentum):
    vmem = pl.BlockSpec(memory_space=pltpu.VMEM)
    return pl.pallas_call(
        base_body,
        out_shape=jax.ShapeDtypeStruct((NX, master.shape[0], 2 * HALF_C), f32),
        in_specs=[pl.BlockSpec(memory_space=pltpu.SMEM), vmem, vmem],
        out_specs=vmem,
        name="base_rows",
    )(at, master, momentum)


def outer_body(at_ref, master_ref, momentum_ref, mean_ref, new_master_ref, new_momentum_ref):
    x, tp = at_ref[0], at_ref[3]
    for quarter in range(NX):
        for half in range(2):
            cols = pl.ds(column_of(tp, half, quarter), HALF_C)
            mean = mean_ref[(quarter - x + NX) % NX, :, half * HALF_C:(half + 1) * HALF_C]
            new = outer_mu * momentum_ref[:, cols] + mean
            new_momentum_ref[:, cols] = new
            new_master_ref[:, cols] = master_ref[:, cols] - outer_rate * (mean + outer_mu * new)


def outer_rows(at, master, momentum, mean):
    vmem = pl.BlockSpec(memory_space=pltpu.VMEM)
    out = jax.ShapeDtypeStruct(master.shape, f32)
    return pl.pallas_call(
        outer_body,
        out_shape=(out, out),
        in_specs=[pl.BlockSpec(memory_space=pltpu.SMEM), vmem, vmem, vmem],
        out_specs=(vmem, vmem),
        name="outer_rows",
    )(at, master, momentum, mean)


def place_body(at_ref, *rest):
    blocks, out_ref, (stage, in_sems, out_sems) = rest[:8], rest[8], rest[9:]
    x, y, zh, tp = at_ref[0], at_ref[1], at_ref[2], at_ref[3]
    copies = []
    for j in range(2):
        for large in range(4):
            for small in range(4):
                ky, kx = (small, large) if j == 0 else (large, small)
                for half in range(2):
                    copies.append(pltpu.make_async_copy(
                        blocks[4 * j + large].at[small, :, half * HALF_C:(half + 1) * HALF_C],
                        stage.at[pl.ds(row_of(zh, y, j, ky), TILE_R),
                                 pl.ds(column_of(tp, half, (x + kx) % NX), HALF_C)],
                        in_sems.at[len(copies)],
                    ))
    for one in copies:
        one.start()
    rows = NY * TILE_R
    outs = []
    for j in range(2):
        for one in copies[32 * j:32 * (j + 1)]:
            one.wait()
        at = pl.ds(pl.multiple_of((zh ^ j) * rows, rows), rows)
        outs.append(pltpu.make_async_copy(stage.at[at], out_ref.at[at], out_sems.at[j]))
        outs[-1].start()
    for one in outs:
        one.wait()


def place(at, blocks, rows, width):
    hbm = pl.BlockSpec(memory_space=pl.ANY)
    return pl.pallas_call(
        place_body,
        out_shape=jax.ShapeDtypeStruct((rows, width), bf16),
        in_specs=[pl.BlockSpec(memory_space=pltpu.SMEM)] + [hbm] * 8,
        out_specs=hbm,
        scratch_shapes=[
            pltpu.VMEM((rows, width), bf16),
            pltpu.SemaphoreType.DMA((64,)),
            pltpu.SemaphoreType.DMA((2,)),
        ],
        compiler_params=pltpu.CompilerParams(vmem_limit_bytes=VMEM_LIMIT),
        name="place",
    )(at, *blocks)


def add(*terms):
    total = terms[0].astype(f32)
    for term in terms[1:]:
        total = total + term.astype(f32)
    return total


def ring(values, axis, sign):
    two = move(values[1], axis, 2 * sign)
    one = move(values[0], axis, sign)
    three = move(values[2], axis, -sign)
    return [one, two, three]


def reduce_blocks(blocks, axis):
    return add(blocks[0], *ring(blocks[1:], axis, 1))


def reduce_tiles(tiles, axis):
    sent = tiles.astype(bf16)
    return add(tiles[0], *ring([sent[1], sent[2], sent[3]], axis, 1))


def rounded(value):
    return lax.reduce_precision(value, 8, 7)


def per_device(queries, keys, values, out_grad, segments, drift, master, momentum):
    tp = lax.axis_index("tp")
    worker = lax.axis_index("worker")
    x, y, zh = worker % NX, (worker // NX) % NY, worker // (NX * NY)
    at = jnp.stack([x, y, zh, tp]).astype(jnp.int32)
    tokens = queries.shape[0]
    own_rows = master.shape[0]
    entries = queries.shape[1] * lax.axis_size("tp") * drift.shape[2]

    across = swap_tp(out_grad, 2)
    partner = swap_tp(out_grad, 1)

    gram = lax.dot_general(out_grad, out_grad, (((1,), (1,)), ((), ())), preferred_element_type=f32)
    side = (tp % 2) * (tokens // 2)
    other = (tokens // 2) - side
    mine = lax.dynamic_slice_in_dim(gram, side, tokens // 2, 0)
    mine = mine + swap_tp(lax.dynamic_slice_in_dim(gram, other, tokens // 2, 0), 1)
    far = swap_tp(mine, 2)

    base = base_rows(at, master, momentum)
    base_got = jnp.stack(
        [lax.dynamic_index_in_dim(base, x, 0, False)]
        + ring([lax.dynamic_index_in_dim(base, (x + k) % NX, 0, False) for k in (1, 2, 3)], "x", 1)
    )
    base_tile = jnp.concatenate(
        [lax.dynamic_index_in_dim(base_got, (x - g + NX) % NX, 0, False) for g in range(NX)], axis=0
    )
    base_tiles = jnp.stack([base_tile, move(base_tile, "z", 1)])

    ct, own_gram = attention(queries, keys, values, segments)
    far, mine, ct, own_gram = lax.optimization_barrier((far, mine, ct, own_gram))
    across, ct = lax.optimization_barrier((across, ct))
    across_partner = swap_tp(across, 1)
    mine = mine + far
    theirs = swap_tp(mine, 1)
    squares = jnp.sum(lax.dynamic_slice_in_dim(own_gram, side, tokens // 2, 0) * mine)
    squares = squares + jnp.sum(lax.dynamic_slice_in_dim(own_gram, other, tokens // 2, 0) * theirs)
    squares = jnp.full((8, 128), squares, f32)
    squares = squares + swap_tp(squares, 1)
    squares = squares + swap_tp(squares, 2)
    scale = (inner_rate / jnp.sqrt(squares[0, :1] / entries + 1e-06))

    scale, base_tiles, across_partner = lax.optimization_barrier((scale, base_tiles, across_partner))
    sends = pseudo_gradient(at, scale, ct, (out_grad, partner, across, across_partner), drift)
    here = reduce_tiles(reduce_blocks(sends[:4], "x"), "y")
    there = reduce_tiles(reduce_blocks(sends[4:], "y"), "x")
    here, there = rounded(here), rounded(there)
    crossed = move(jnp.stack([there, here]).astype(bf16), "z", 1)
    mean = (jnp.stack([here, there]) + crossed.astype(f32)) / lax.axis_size("worker")
    fresh = (base_tiles - (outer_rate * (1.0 + outer_mu)) * mean).astype(bf16)

    def mean_rows(k):
        return lax.dynamic_slice_in_dim(mean[0], ((x + k) % NX) * own_rows, own_rows, 0)

    here_got = ring([fresh[0]] * 3, "y", -1)
    there_got = ring(
        [jnp.concatenate([fresh[1], mean_rows(NX - k).astype(bf16)]) for k in (1, 2, 3)], "x", -1
    )
    means = jnp.stack([mean_rows(0)] + [got[TILE_R:].astype(f32) for got in there_got])
    here_block = jnp.stack([fresh[0]] + here_got)
    there_block = jnp.stack([fresh[1]] + [got[:TILE_R] for got in there_got])
    here_blocks = [here_block] + ring([here_block] * 3, "x", -1)
    there_blocks = [there_block] + ring([there_block] * 3, "y", -1)
    new_master, new_momentum = outer_rows(at, master, momentum, means)
    new_params = place(at, here_blocks + there_blocks, drift.shape[1], drift.shape[2])
    return (new_params, new_master, new_momentum)


def solution(mesh):
    placed = (
        P("worker", "tp"),
        P("worker", "tp"),
        P("worker", "tp"),
        P("worker", "tp"),
        P("worker"),
        P("worker", "tp", None),
        P(("tp", "worker"), None),
        P(("tp", "worker"), None),
    )
    return jax.shard_map(
        per_device,
        mesh=mesh,
        in_specs=placed,
        out_specs=(P("tp", None), P(("tp", "worker"), None), P(("tp", "worker"), None)),
        check_vma=False,
    )
```

```python
import functools
import math

import jax
import jax.numpy as jnp
from jax import lax
from jax.experimental import pallas as pl
from jax.experimental.pallas import tpu as pltpu
from jax.sharding import PartitionSpec as P

HD = 128
NX, NY, NZ = 4, 4, 2
TILE_R = 80
HALF_C = 640

inner_rate = 0.8
outer_rate = 0.7
outer_mu = 0.9
neg_big = -1e30
bf16 = jnp.bfloat16
f32 = jnp.float32
VMEM_LIMIT = 60 << 20


def worker_of(zh, y, x):
    return (zh % NZ) * NX * NY + (y % NY) * NX + (x % NX)


def move(value, axis, step):
    pairs = []
    for zh in range(NZ):
        for y in range(NY):
            for x in range(NX):
                to = {
                    "x": worker_of(zh, y, x + step),
                    "y": worker_of(zh, y + step, x),
                    "z": worker_of(zh + step, y, x),
                }[axis]
                pairs.append((worker_of(zh, y, x), to))
    return lax.ppermute(value, "worker", pairs)


def swap_tp(value, bit):
    return lax.ppermute(value, "tp", [(t, t ^ bit) for t in range(4)])


LOWER = [(i, j) for i in range(3) for j in range(i + 1)]


def cotangent_gram_body(grad_ref, gram_ref):
    for n, (i, j) in enumerate(LOWER):
        gram_ref[n] = lax.dot_general(
            grad_ref[i * HD:(i + 1) * HD, :], grad_ref[j * HD:(j + 1) * HD, :],
            (((1,), (1,)), ((), ())), preferred_element_type=f32,
        )


def cotangent_gram(grad):
    return pl.pallas_call(
        cotangent_gram_body,
        out_shape=jax.ShapeDtypeStruct((len(LOWER), HD, HD), f32),
        name="cotangent_gram",
    )(grad)


def attention_body(q_ref, k_ref, v_ref, seg_row_ref, ct_ref, gram_ref):
    tokens, width = q_ref.shape
    scale = 1.0 / math.sqrt(HD)
    blocks = tokens // HD
    seg_row = seg_row_ref[...]
    seg_col = jnp.broadcast_to(seg_row.astype(f32), (HD, tokens)).T.astype(jnp.int32)
    for h in range(width // HD):
        cols = slice(h * HD, (h + 1) * HD)
        for b in range(blocks):
            queries = slice(b * HD, (b + 1) * HD)
            seen = (b + 1) * HD
            scores = lax.dot_general(
                k_ref[:seen, cols], q_ref[queries, cols], (((1,), (1,)), ((), ())),
                preferred_element_type=f32,
            ) * scale
            key_at = lax.broadcasted_iota(jnp.int32, (seen, HD), 0)
            query_at = lax.broadcasted_iota(jnp.int32, (seen, HD), 1) + b * HD
            allowed = (key_at <= query_at) & (seg_col[:seen, :] == seg_row[:, queries])
            scores = jnp.where(allowed, scores, neg_big)
            exp_scores = jnp.exp(scores - jnp.max(scores, axis=0, keepdims=True))
            total = jnp.sum(exp_scores, axis=0, keepdims=True)
            weights = (exp_scores * (1.0 / total)).astype(bf16)
            ct_ref[cols, queries] = lax.dot_general(
                v_ref[:seen, cols], weights, (((0,), (0,)), ((), ())),
                preferred_element_type=f32,
            ).astype(bf16)
    for n, (i, j) in enumerate(LOWER):
        block = lax.dot_general(
            ct_ref[:, i * HD:(i + 1) * HD], ct_ref[:, j * HD:(j + 1) * HD],
            (((0,), (0,)), ((), ())), preferred_element_type=f32,
        )
        gram_ref[n] = block if i == j else 2.0 * block


def attention(queries, keys, values, segments):
    tokens, width = queries.shape
    return pl.pallas_call(
        attention_body,
        out_shape=(
            jax.ShapeDtypeStruct((width, tokens), bf16),
            jax.ShapeDtypeStruct((len(LOWER), HD, HD), f32),
        ),
        compiler_params=pltpu.CompilerParams(vmem_limit_bytes=VMEM_LIMIT),
        name="attention",
    )(queries, keys, values, segments.reshape(1, tokens))


def column_of(tp, half, quarter):
    first = (tp ^ (2 * half) ^ (quarter // 2)) * (2 * HALF_C) + (quarter % 2) * HALF_C
    return pl.multiple_of(first, HALF_C)


def row_of(zh, y, j, ky):
    return pl.multiple_of((zh ^ j) * (NY * TILE_R) + ((y + ky) % NY) * TILE_R, TILE_R)


K_ORDER = (2, 1, 3, 0)
UP_DOWN = ((2, 2, 1, 1), (3, 3, 2, 2))
FIRST = [[(0, n, far[n]) for n in range(4)] for far in UP_DOWN] + [
    [(1, far[n], n) for n in range(4)] for far in UP_DOWN
]
LATER = [
    [(0, n, 0) for n in range(4)], [(0, 0, 1), (0, 1, 1)], [(0, 2, 3), (0, 3, 3)],
    [(1, 0, n) for n in range(4)], [(1, 1, 0), (1, 1, 1)], [(1, 3, 2), (1, 3, 3)],
]


def pseudo_body(outputs, at_ref, scale_ref, ct_ref, g0_ref, g1_ref, g2_ref, g3_ref, drift_ref, *rest):
    outs = rest[:len(outputs)]
    drift_buf, g_buf, rows_buf, out_buf, drift_sems, g_sems, out_sems = rest[len(outputs):]
    x, y, zh, tp = at_ref[0], at_ref[1], at_ref[2], at_ref[3]
    scale = scale_ref[0]
    pieces = ((g0_ref, g1_ref), (g2_ref, g3_ref))

    def g_copy(slot, ref, k):
        return pltpu.make_async_copy(
            ref.at[:, pl.ds(pl.multiple_of(((x + k) % 2) * HALF_C, HALF_C), HALF_C)],
            g_buf.at[slot], g_sems.at[slot],
        )

    def g_start(slot, ref, k):
        g_copy(slot, ref, k).start()

    def drift_copy(slot, k, half):
        return pltpu.make_async_copy(
            drift_ref.at[0, :, pl.ds(column_of(tp, half, (x + k) % NX), HALF_C)],
            drift_buf.at[slot], drift_sems.at[slot],
        )

    steps = [(k, half) for k in K_ORDER for half in range(2)]
    for slot, (k, half) in enumerate(steps):
        for side, ref in enumerate(pieces[half]):
            pl.when(((x + k) % NX) // 2 == side)(functools.partial(g_start, slot, ref, k))
        drift_copy(slot, k, half).start()
    for j in range(2):
        for ky in range(NY):
            first = (j * NY + ky) * TILE_R
            rows_buf[first:first + TILE_R, :] = ct_ref[pl.ds(row_of(zh, y, j, ky), TILE_R), :]

    copies = []
    for slot, (k, half) in enumerate(steps):
        cols = slice(half * HALF_C, (half + 1) * HALF_C)
        g_copy(slot, g0_ref, k).wait()
        drift_copy(slot, k, half).wait()
        for j in range(2):
            rows = slice(j * NY * TILE_R, (j + 1) * NY * TILE_R)
            block = jnp.dot(rows_buf[rows, :], g_buf[slot], preferred_element_type=f32)
            for ky in range(NY):
                own = drift_buf[slot, pl.ds(row_of(zh, y, j, ky), TILE_R), :]
                value = block[ky * TILE_R:(ky + 1) * TILE_R] * scale + own.astype(f32)
                out_buf[k, j * NY + ky, :, cols] = value.astype(bf16)
        if half == 1:
            for j in range(2):
                for ky in range(NY):
                    o, index = next(
                        (o, tiles.index((j, ky, k))) for o, tiles in enumerate(outputs) if (j, ky, k) in tiles
                    )
                    copies.append(pltpu.make_async_copy(
                        out_buf.at[k, j * NY + ky], outs[o].at[index], out_sems.at[len(copies)]
                    ))
                    copies[-1].start()
    for one in copies:
        one.wait()


def pseudo_gradient(outputs, name, at, scale, ct, pieces, drift):
    smem = pl.BlockSpec(memory_space=pltpu.SMEM)
    hbm = pl.BlockSpec(memory_space=pl.ANY)
    tokens, rows = ct.shape[1], ct.shape[0]
    count = sum(len(tiles) for tiles in outputs)
    return pl.pallas_call(
        functools.partial(pseudo_body, outputs),
        out_shape=tuple(
            jax.ShapeDtypeStruct((len(tiles), TILE_R, 2 * HALF_C), bf16) for tiles in outputs
        ),
        in_specs=[smem, smem, pl.BlockSpec(memory_space=pltpu.VMEM)] + [hbm] * 5,
        out_specs=(hbm,) * len(outputs),
        scratch_shapes=[
            pltpu.VMEM((8, rows, HALF_C), bf16),
            pltpu.VMEM((8, tokens, HALF_C), bf16),
            pltpu.VMEM(ct.shape, bf16),
            pltpu.VMEM((NX, 2 * NY, TILE_R, 2 * HALF_C), bf16),
            pltpu.SemaphoreType.DMA((8,)),
            pltpu.SemaphoreType.DMA((8,)),
            pltpu.SemaphoreType.DMA((count,)),
        ],
        compiler_params=pltpu.CompilerParams(vmem_limit_bytes=VMEM_LIMIT),
        cost_estimate=pl.CostEstimate(
            flops=2 * rows * tokens * 5120, bytes_accessed=18_000_000, transcendentals=0
        ),
        name=name,
    )(at, scale, ct, *pieces, drift)


def base_body(at_ref, master_ref, momentum_ref, base_ref):
    tp = at_ref[3]
    for quarter in range(NX):
        for half in range(2):
            cols = pl.ds(column_of(tp, half, quarter), HALF_C)
            base_ref[quarter, :, half * HALF_C:(half + 1) * HALF_C] = (
                master_ref[:, cols] - (outer_rate * outer_mu * outer_mu) * momentum_ref[:, cols]
            )


def base_rows(at, master, momentum):
    vmem = pl.BlockSpec(memory_space=pltpu.VMEM)
    return pl.pallas_call(
        base_body,
        out_shape=jax.ShapeDtypeStruct((NX, master.shape[0], 2 * HALF_C), f32),
        in_specs=[pl.BlockSpec(memory_space=pltpu.SMEM), vmem, vmem],
        out_specs=vmem,
        name="base_rows",
    )(at, master, momentum)


def outer_body(at_ref, master_ref, momentum_ref, mean_ref, new_master_ref, new_momentum_ref):
    x, tp = at_ref[0], at_ref[3]
    for quarter in range(NX):
        for half in range(2):
            cols = pl.ds(column_of(tp, half, quarter), HALF_C)
            mean = mean_ref[(quarter - x + NX) % NX, :, half * HALF_C:(half + 1) * HALF_C]
            new = outer_mu * momentum_ref[:, cols] + mean
            new_momentum_ref[:, cols] = new
            new_master_ref[:, cols] = master_ref[:, cols] - outer_rate * (mean + outer_mu * new)


def outer_rows(at, master, momentum, mean):
    vmem = pl.BlockSpec(memory_space=pltpu.VMEM)
    out = jax.ShapeDtypeStruct(master.shape, f32)
    return pl.pallas_call(
        outer_body,
        out_shape=(out, out),
        in_specs=[pl.BlockSpec(memory_space=pltpu.SMEM), vmem, vmem, vmem],
        out_specs=(vmem, vmem),
        name="outer_rows",
    )(at, master, momentum, mean)


def place_body(where, at_ref, *rest):
    count = len(where)
    blocks, (out_ref, stage, in_sems, out_sems) = rest[:count], rest[-4:]
    x, y, zh, tp = at_ref[0], at_ref[1], at_ref[2], at_ref[3]
    slots = [sum(len(tiles) for tiles in where[:n]) for n in range(count)]
    loads = [
        pltpu.make_async_copy(blocks[n], stage.at[slots[n]:slots[n] + len(where[n])], in_sems.at[n])
        for n in range(count)
    ]
    for one in loads:
        one.start()
    stores = []
    for n, tiles in enumerate(where):
        loads[n].wait()
        for m, (j, ky, k) in enumerate(tiles):
            for half in range(2):
                stores.append(pltpu.make_async_copy(
                    stage.at[slots[n] + m, :, half * HALF_C:(half + 1) * HALF_C],
                    out_ref.at[pl.ds(row_of(zh, y, j, ky), TILE_R),
                               pl.ds(column_of(tp, half, (x + k) % NX), HALF_C)],
                    out_sems.at[len(stores)],
                ))
                stores[-1].start()
    for one in stores:
        one.wait()


def place(name, where, at, blocks, rows, width, so_far=None):
    hbm = pl.BlockSpec(memory_space=pl.ANY)
    count = sum(len(tiles) for tiles in where)
    operands = [at, *blocks] + ([] if so_far is None else [so_far])
    return pl.pallas_call(
        functools.partial(place_body, where),
        out_shape=jax.ShapeDtypeStruct((rows, width), bf16),
        in_specs=[pl.BlockSpec(memory_space=pltpu.SMEM)] + [hbm] * (len(operands) - 1),
        out_specs=hbm,
        scratch_shapes=[
            pltpu.VMEM((count, TILE_R, 2 * HALF_C), bf16),
            pltpu.SemaphoreType.DMA((len(where),)),
            pltpu.SemaphoreType.DMA((2 * count,)),
        ],
        input_output_aliases={} if so_far is None else {len(operands) - 1: 0},
        compiler_params=pltpu.CompilerParams(vmem_limit_bytes=VMEM_LIMIT),
        cost_estimate=pl.CostEstimate(
            flops=0, bytes_accessed=4 * count * TILE_R * 2 * HALF_C, transcendentals=0
        ),
        name=name,
    )(*operands)


def add(*terms):
    total = terms[0].astype(f32)
    for term in terms[1:]:
        total = total + term.astype(f32)
    return total


def ring(values, axis, sign):
    two = move(values[1], axis, 2 * sign)
    one = move(values[0], axis, sign)
    three = move(values[2], axis, -sign)
    return [one, two, three]


def pass_on(waves, later, axis):
    up, down = move(waves[0], axis, 1), move(waves[1], axis, -1)
    onward_up = add(later[1], up[:2]).astype(bf16)
    onward_down = add(later[2], down[2:]).astype(bf16)
    return up, down, onward_up, onward_down


def arrive(own, up, down, onward_up, onward_down, axis):
    last_up, last_down = move(onward_up, axis, 1), move(onward_down, axis, -1)
    low = add(own[:2], down[:2], last_up)
    high = add(own[2:], up[2:], last_down)
    return jnp.concatenate([low, high])


def reduce_tiles(tiles, axis):
    sent = tiles.astype(bf16)
    return add(tiles[0], *ring([sent[1], sent[2], sent[3]], axis, 1))


def per_device(queries, keys, values, out_grad, segments, drift, master, momentum):
    tp = lax.axis_index("tp")
    worker = lax.axis_index("worker")
    x, y, zh = worker % NX, (worker // NX) % NY, worker // (NX * NY)
    at = jnp.stack([x, y, zh, tp]).astype(jnp.int32)
    own_rows = master.shape[0]
    entries = queries.shape[1] * lax.axis_size("tp") * drift.shape[2]

    partner = swap_tp(out_grad, 1)

    packed = cotangent_gram(out_grad)
    side = (tp % 2) * 3
    mine = lax.dynamic_slice_in_dim(packed, side, 3, 0)
    mine = mine + swap_tp(lax.dynamic_slice_in_dim(packed, 3 - side, 3, 0), 1)
    far = swap_tp(mine, 2)

    mine, queries = lax.optimization_barrier((mine, queries))
    ct, own_gram = attention(queries, keys, values, segments)
    far, crossing = lax.optimization_barrier((far, out_grad))
    across = swap_tp(crossing, 2)
    ct, early_at = lax.optimization_barrier((ct, at))
    base = base_rows(early_at, master, momentum)
    rings = [[first + n for n in range(NX)] for first in range(0, NX * NY * NZ, NX)]
    base_tile = lax.all_to_all(base, "worker", 0, 0, axis_index_groups=rings)
    base_tile = base_tile.reshape(TILE_R, 2 * HALF_C)
    far, mine, ct, own_gram = lax.optimization_barrier((far, mine, ct, own_gram))
    mine = mine + far
    theirs = swap_tp(mine, 1)
    squares = jnp.sum(lax.dynamic_slice_in_dim(own_gram, side, 3, 0) * mine)
    squares = squares + jnp.sum(lax.dynamic_slice_in_dim(own_gram, 3 - side, 3, 0) * theirs)
    squares = jnp.full((8, 128), squares, f32)
    squares = squares + swap_tp(squares, 1)
    across, base_tile, squares = lax.optimization_barrier((across, base_tile, squares))
    across_partner = swap_tp(across, 1)
    squares = squares + swap_tp(squares, 2)
    scale = (inner_rate / jnp.sqrt(squares[0, :1] / entries + 1e-06))

    pieces = (out_grad, partner, across, across_partner)
    scale, base_tile = lax.optimization_barrier((scale, base_tile))
    sends = pseudo_gradient(FIRST + LATER, "pseudo_gradient", at, scale, ct, pieces, drift)
    waves, later = sends[:4], sends[4:]
    here, there = pass_on(waves[:2], later[:3], "x"), pass_on(waves[2:], later[3:], "y")
    there, base_tile = lax.optimization_barrier((there, base_tile))
    base_tiles = jnp.stack([base_tile, move(base_tile, "z", 1)])
    here, there = arrive(later[0], *here, "x"), arrive(later[3], *there, "y")
    here, there = reduce_tiles(here, "y"), reduce_tiles(there, "x")
    here, there = lax.reduce_precision(here, 8, 7), lax.reduce_precision(there, 8, 7)
    crossed = move(jnp.stack([there, here]).astype(bf16), "z", 1)
    means = (jnp.stack([here, there]) + crossed.astype(f32)) / lax.axis_size("worker")
    fresh = (base_tiles - (outer_rate * (1.0 + outer_mu)) * means).astype(bf16)
    mean, tile, opposite = means[0], fresh[0], fresh[1]

    def mean_rows(k):
        return lax.dynamic_slice_in_dim(mean, ((x + k) % NX) * own_rows, own_rows, 0)

    here_got = ring([tile] * 3, "y", -1)
    there_got = ring(
        [jnp.concatenate([opposite, mean_rows(NX - k).astype(bf16)]) for k in (1, 2, 3)], "x", -1
    )
    means = jnp.stack([mean_rows(0)] + [got[TILE_R:].astype(f32) for got in there_got])
    there_got = [got[:TILE_R] for got in there_got]
    here = jnp.stack([tile] + here_got)
    there = jnp.stack([opposite] + there_got)
    here, there, means = lax.optimization_barrier((here, there, means))
    here_1, here_3 = move(here, "x", -1), move(here, "x", 1)
    there_1, there_3 = move(there, "y", -1), move(there, "y", 1)
    last = [
        move(here_1[:2], "x", -1), move(here_3[2:], "x", 1),
        move(there_1[:2], "y", -1), move(there_3[2:], "y", 1),
    ]
    new_master, new_momentum = outer_rows(at, master, momentum, means)
    rows, width = drift.shape[1], drift.shape[2]
    so_far = place(
        "place_first",
        [[(0, n, k) for n in range(4)] for k in (0, 1, 3)] + [[(1, ky, n) for n in range(4)] for ky in (0, 1, 3)],
        at, [here, here_1, here_3, there, there_1, there_3], rows, width,
    )
    new_params = place(
        "place_last",
        [[(0, 0, 2), (0, 1, 2)], [(0, 2, 2), (0, 3, 2)], [(1, 2, 0), (1, 2, 1)], [(1, 2, 2), (1, 2, 3)]],
        at, last, rows, width, so_far,
    )
    return (new_params, new_master, new_momentum)


def solution(mesh):
    placed = (
        P("worker", "tp"),
        P("worker", "tp"),
        P("worker", "tp"),
        P("worker", "tp"),
        P("worker"),
        P("worker", "tp", None),
        P(("tp", "worker"), None),
        P(("tp", "worker"), None),
    )
    return jax.shard_map(
        per_device,
        mesh=mesh,
        in_specs=placed,
        out_specs=(P("tp", None), P(("tp", "worker"), None), P(("tp", "worker"), None)),
        check_vma=False,
    )
```

```python
import functools
import math

import jax
import jax.numpy as jnp
from jax import lax
from jax.experimental import pallas as pl
from jax.experimental.pallas import tpu as pltpu
from jax.sharding import PartitionSpec as P

HD = 128
NX, NY, NZ = 4, 4, 2
TILE_R = 80
HALF_C = 640

inner_rate = 0.8
outer_rate = 0.7
outer_mu = 0.9
neg_big = -1e30
bf16 = jnp.bfloat16
f32 = jnp.float32
VMEM_LIMIT = 60 << 20


def worker_of(zh, y, x):
    return (zh % NZ) * NX * NY + (y % NY) * NX + (x % NX)


def move(value, axis, step):
    pairs = []
    for zh in range(NZ):
        for y in range(NY):
            for x in range(NX):
                to = {
                    "x": worker_of(zh, y, x + step),
                    "y": worker_of(zh, y + step, x),
                    "z": worker_of(zh + step, y, x),
                }[axis]
                pairs.append((worker_of(zh, y, x), to))
    return lax.ppermute(value, "worker", pairs)


def swap_tp(value, bit):
    return lax.ppermute(value, "tp", [(t, t ^ bit) for t in range(4)])


LOWER = [(i, j) for i in range(3) for j in range(i + 1)]


def cotangent_gram_body(grad_ref, gram_ref):
    for n, (i, j) in enumerate(LOWER):
        gram_ref[n] = lax.dot_general(
            grad_ref[i * HD:(i + 1) * HD, :], grad_ref[j * HD:(j + 1) * HD, :],
            (((1,), (1,)), ((), ())), preferred_element_type=f32,
        )


def cotangent_gram(grad):
    return pl.pallas_call(
        cotangent_gram_body,
        out_shape=jax.ShapeDtypeStruct((len(LOWER), HD, HD), f32),
        name="cotangent_gram",
    )(grad)


def attention_body(q_ref, k_ref, v_ref, seg_row_ref, ct_ref, gram_ref):
    tokens, width = q_ref.shape
    scale = 1.0 / math.sqrt(HD)
    blocks = tokens // HD
    seg_row = seg_row_ref[...]
    seg_col = jnp.broadcast_to(seg_row.astype(f32), (HD, tokens)).T.astype(jnp.int32)
    for h in range(width // HD):
        cols = slice(h * HD, (h + 1) * HD)
        for b in range(blocks):
            queries = slice(b * HD, (b + 1) * HD)
            seen = (b + 1) * HD
            scores = lax.dot_general(
                k_ref[:seen, cols], q_ref[queries, cols], (((1,), (1,)), ((), ())),
                preferred_element_type=f32,
            ) * scale
            key_at = lax.broadcasted_iota(jnp.int32, (seen, HD), 0)
            query_at = lax.broadcasted_iota(jnp.int32, (seen, HD), 1) + b * HD
            allowed = (key_at <= query_at) & (seg_col[:seen, :] == seg_row[:, queries])
            scores = jnp.where(allowed, scores, neg_big)
            exp_scores = jnp.exp(scores - jnp.max(scores, axis=0, keepdims=True))
            total = jnp.sum(exp_scores, axis=0, keepdims=True)
            weights = (exp_scores * (1.0 / total)).astype(bf16)
            ct_ref[cols, queries] = lax.dot_general(
                v_ref[:seen, cols], weights, (((0,), (0,)), ((), ())),
                preferred_element_type=f32,
            ).astype(bf16)
    for n, (i, j) in enumerate(LOWER):
        block = lax.dot_general(
            ct_ref[:, i * HD:(i + 1) * HD], ct_ref[:, j * HD:(j + 1) * HD],
            (((0,), (0,)), ((), ())), preferred_element_type=f32,
        )
        gram_ref[n] = block if i == j else 2.0 * block


def attention(queries, keys, values, segments):
    tokens, width = queries.shape
    return pl.pallas_call(
        attention_body,
        out_shape=(
            jax.ShapeDtypeStruct((width, tokens), bf16),
            jax.ShapeDtypeStruct((len(LOWER), HD, HD), f32),
        ),
        compiler_params=pltpu.CompilerParams(vmem_limit_bytes=VMEM_LIMIT),
        name="attention",
    )(queries, keys, values, segments.reshape(1, tokens))


def column_of(tp, half, quarter):
    first = (tp ^ (2 * half) ^ (quarter // 2)) * (2 * HALF_C) + (quarter % 2) * HALF_C
    return pl.multiple_of(first, HALF_C)


def row_of(zh, y, j, ky):
    return pl.multiple_of((zh ^ j) * (NY * TILE_R) + ((y + ky) % NY) * TILE_R, TILE_R)


K_ORDER = (2, 1, 3, 0)
UP_DOWN = ((2, 2, 1, 1), (3, 3, 2, 2))
FIRST = [[(0, n, far[n]) for n in range(4)] for far in UP_DOWN] + [
    [(1, far[n], n) for n in range(4)] for far in UP_DOWN
]
LATER = [
    [(0, n, 0) for n in range(4)], [(0, 0, 1), (0, 1, 1)], [(0, 2, 3), (0, 3, 3)],
    [(1, 0, n) for n in range(4)], [(1, 1, 0), (1, 1, 1)], [(1, 3, 2), (1, 3, 3)],
]


def pseudo_body(outputs, at_ref, scale_ref, ct_ref, g0_ref, g1_ref, g2_ref, g3_ref, drift_ref, *rest):
    outs = rest[:len(outputs)]
    drift_buf, g_buf, rows_buf, out_buf, drift_sems, g_sems, out_sems = rest[len(outputs):]
    x, y, zh, tp = at_ref[0], at_ref[1], at_ref[2], at_ref[3]
    scale = scale_ref[0]
    pieces = ((g0_ref, g1_ref), (g2_ref, g3_ref))

    def g_copy(slot, ref, k):
        return pltpu.make_async_copy(
            ref.at[:, pl.ds(pl.multiple_of(((x + k) % 2) * HALF_C, HALF_C), HALF_C)],
            g_buf.at[slot], g_sems.at[slot],
        )

    def g_start(slot, ref, k):
        g_copy(slot, ref, k).start()

    def drift_copy(slot, k, half):
        return pltpu.make_async_copy(
            drift_ref.at[0, :, pl.ds(column_of(tp, half, (x + k) % NX), HALF_C)],
            drift_buf.at[slot], drift_sems.at[slot],
        )

    steps = [(k, half) for k in K_ORDER for half in range(2)]
    for slot, (k, half) in enumerate(steps):
        for side, ref in enumerate(pieces[half]):
            pl.when(((x + k) % NX) // 2 == side)(functools.partial(g_start, slot, ref, k))
        drift_copy(slot, k, half).start()
    for j in range(2):
        for ky in range(NY):
            first = (j * NY + ky) * TILE_R
            rows_buf[first:first + TILE_R, :] = ct_ref[pl.ds(row_of(zh, y, j, ky), TILE_R), :]

    copies = []
    for slot, (k, half) in enumerate(steps):
        cols = slice(half * HALF_C, (half + 1) * HALF_C)
        g_copy(slot, g0_ref, k).wait()
        drift_copy(slot, k, half).wait()
        for j in range(2):
            rows = slice(j * NY * TILE_R, (j + 1) * NY * TILE_R)
            block = jnp.dot(rows_buf[rows, :], g_buf[slot], preferred_element_type=f32)
            for ky in range(NY):
                own = drift_buf[slot, pl.ds(row_of(zh, y, j, ky), TILE_R), :]
                value = block[ky * TILE_R:(ky + 1) * TILE_R] * scale + own.astype(f32)
                out_buf[k, j * NY + ky, :, cols] = value.astype(bf16)
        if half == 1:
            for j in range(2):
                for ky in range(NY):
                    o, index = next(
                        (o, tiles.index((j, ky, k))) for o, tiles in enumerate(outputs) if (j, ky, k) in tiles
                    )
                    copies.append(pltpu.make_async_copy(
                        out_buf.at[k, j * NY + ky], outs[o].at[index], out_sems.at[len(copies)]
                    ))
                    copies[-1].start()
    for one in copies:
        one.wait()


def pseudo_gradient(outputs, name, at, scale, ct, pieces, drift):
    smem = pl.BlockSpec(memory_space=pltpu.SMEM)
    hbm = pl.BlockSpec(memory_space=pl.ANY)
    tokens, rows = ct.shape[1], ct.shape[0]
    count = sum(len(tiles) for tiles in outputs)
    return pl.pallas_call(
        functools.partial(pseudo_body, outputs),
        out_shape=tuple(
            jax.ShapeDtypeStruct((len(tiles), TILE_R, 2 * HALF_C), bf16) for tiles in outputs
        ),
        in_specs=[smem, smem, pl.BlockSpec(memory_space=pltpu.VMEM)] + [hbm] * 5,
        out_specs=(hbm,) * len(outputs),
        scratch_shapes=[
            pltpu.VMEM((8, rows, HALF_C), bf16),
            pltpu.VMEM((8, tokens, HALF_C), bf16),
            pltpu.VMEM(ct.shape, bf16),
            pltpu.VMEM((NX, 2 * NY, TILE_R, 2 * HALF_C), bf16),
            pltpu.SemaphoreType.DMA((8,)),
            pltpu.SemaphoreType.DMA((8,)),
            pltpu.SemaphoreType.DMA((count,)),
        ],
        compiler_params=pltpu.CompilerParams(vmem_limit_bytes=VMEM_LIMIT),
        cost_estimate=pl.CostEstimate(
            flops=2 * rows * tokens * 5120, bytes_accessed=18_000_000, transcendentals=0
        ),
        name=name,
    )(at, scale, ct, *pieces, drift)


def base_body(at_ref, master_ref, momentum_ref, base_ref):
    tp = at_ref[3]
    for quarter in range(NX):
        for half in range(2):
            cols = pl.ds(column_of(tp, half, quarter), HALF_C)
            base_ref[quarter, :, half * HALF_C:(half + 1) * HALF_C] = (
                master_ref[:, cols] - (outer_rate * outer_mu * outer_mu) * momentum_ref[:, cols]
            )


def base_rows(at, master, momentum):
    vmem = pl.BlockSpec(memory_space=pltpu.VMEM)
    return pl.pallas_call(
        base_body,
        out_shape=jax.ShapeDtypeStruct((NX, master.shape[0], 2 * HALF_C), f32),
        in_specs=[pl.BlockSpec(memory_space=pltpu.SMEM), vmem, vmem],
        out_specs=vmem,
        name="base_rows",
    )(at, master, momentum)


def outer_body(at_ref, master_ref, momentum_ref, mean_ref, new_master_ref, new_momentum_ref):
    x, tp = at_ref[0], at_ref[3]
    for quarter in range(NX):
        for half in range(2):
            cols = pl.ds(column_of(tp, half, quarter), HALF_C)
            mean = mean_ref[(quarter - x + NX) % NX, :, half * HALF_C:(half + 1) * HALF_C]
            new = outer_mu * momentum_ref[:, cols] + mean
            new_momentum_ref[:, cols] = new
            new_master_ref[:, cols] = master_ref[:, cols] - outer_rate * (mean + outer_mu * new)


def outer_rows(at, master, momentum, mean):
    vmem = pl.BlockSpec(memory_space=pltpu.VMEM)
    out = jax.ShapeDtypeStruct(master.shape, f32)
    return pl.pallas_call(
        outer_body,
        out_shape=(out, out),
        in_specs=[pl.BlockSpec(memory_space=pltpu.SMEM), vmem, vmem, vmem],
        out_specs=(vmem, vmem),
        name="outer_rows",
    )(at, master, momentum, mean)


def place_body(where, at_ref, *rest):
    count = len(where)
    blocks, (out_ref, stage, in_sems, out_sems) = rest[:count], rest[-4:]
    x, y, zh, tp = at_ref[0], at_ref[1], at_ref[2], at_ref[3]
    slots = [sum(len(tiles) for tiles in where[:n]) for n in range(count)]
    loads = [
        pltpu.make_async_copy(blocks[n], stage.at[slots[n]:slots[n] + len(where[n])], in_sems.at[n])
        for n in range(count)
    ]
    for one in loads:
        one.start()
    stores = []
    for n, tiles in enumerate(where):
        loads[n].wait()
        for m, (j, ky, k) in enumerate(tiles):
            for half in range(2):
                stores.append(pltpu.make_async_copy(
                    stage.at[slots[n] + m, :, half * HALF_C:(half + 1) * HALF_C],
                    out_ref.at[pl.ds(row_of(zh, y, j, ky), TILE_R),
                               pl.ds(column_of(tp, half, (x + k) % NX), HALF_C)],
                    out_sems.at[len(stores)],
                ))
                stores[-1].start()
    for one in stores:
        one.wait()


def place(name, where, at, blocks, rows, width, so_far=None):
    hbm = pl.BlockSpec(memory_space=pl.ANY)
    count = sum(len(tiles) for tiles in where)
    operands = [at, *blocks] + ([] if so_far is None else [so_far])
    return pl.pallas_call(
        functools.partial(place_body, where),
        out_shape=jax.ShapeDtypeStruct((rows, width), bf16),
        in_specs=[pl.BlockSpec(memory_space=pltpu.SMEM)] + [hbm] * (len(operands) - 1),
        out_specs=hbm,
        scratch_shapes=[
            pltpu.VMEM((count, TILE_R, 2 * HALF_C), bf16),
            pltpu.SemaphoreType.DMA((len(where),)),
            pltpu.SemaphoreType.DMA((2 * count,)),
        ],
        input_output_aliases={} if so_far is None else {len(operands) - 1: 0},
        compiler_params=pltpu.CompilerParams(vmem_limit_bytes=VMEM_LIMIT),
        cost_estimate=pl.CostEstimate(
            flops=0, bytes_accessed=4 * count * TILE_R * 2 * HALF_C, transcendentals=0
        ),
        name=name,
    )(*operands)


def add(*terms):
    total = terms[0].astype(f32)
    for term in terms[1:]:
        total = total + term.astype(f32)
    return total


def ring(values, axis, sign):
    two = move(values[1], axis, 2 * sign)
    one = move(values[0], axis, sign)
    three = move(values[2], axis, -sign)
    return [one, two, three]


def pass_on(waves, later, axis):
    up, down = move(waves[0], axis, 1), move(waves[1], axis, -1)
    onward_up = add(later[1], up[:2]).astype(bf16)
    onward_down = add(later[2], down[2:]).astype(bf16)
    return up, down, onward_up, onward_down


def arrive(own, up, down, onward_up, onward_down, axis):
    last_up, last_down = move(onward_up, axis, 1), move(onward_down, axis, -1)
    low = add(own[:2], down[:2], last_up)
    high = add(own[2:], up[2:], last_down)
    return jnp.concatenate([low, high])


def reduce_tiles(tiles, axis):
    sent = tiles.astype(bf16)
    return add(tiles[0], *ring([sent[1], sent[2], sent[3]], axis, 1))


def per_device(queries, keys, values, out_grad, segments, drift, master, momentum):
    tp = lax.axis_index("tp")
    worker = lax.axis_index("worker")
    x, y, zh = worker % NX, (worker // NX) % NY, worker // (NX * NY)
    at = jnp.stack([x, y, zh, tp]).astype(jnp.int32)
    own_rows = master.shape[0]
    entries = queries.shape[1] * lax.axis_size("tp") * drift.shape[2]

    partner = swap_tp(out_grad, 1)

    packed = cotangent_gram(out_grad)
    side = (tp % 2) * 3
    mine = lax.dynamic_slice_in_dim(packed, side, 3, 0)
    mine = mine + swap_tp(lax.dynamic_slice_in_dim(packed, 3 - side, 3, 0), 1)
    far = swap_tp(mine, 2)

    mine, queries = lax.optimization_barrier((mine, queries))
    ct, own_gram = attention(queries, keys, values, segments)
    far, crossing = lax.optimization_barrier((far, out_grad))
    across = swap_tp(crossing, 2)
    ct, early_at = lax.optimization_barrier((ct, at))
    base = base_rows(early_at, master, momentum)
    rings = [[first + n for n in range(NX)] for first in range(0, NX * NY * NZ, NX)]
    base_tile = lax.all_to_all(base, "worker", 0, 0, axis_index_groups=rings)
    base_tile = base_tile.reshape(TILE_R, 2 * HALF_C)
    far, mine, ct, own_gram = lax.optimization_barrier((far, mine, ct, own_gram))
    mine = mine + far
    theirs = swap_tp(mine, 1)
    squares = jnp.sum(lax.dynamic_slice_in_dim(own_gram, side, 3, 0) * mine)
    squares = squares + jnp.sum(lax.dynamic_slice_in_dim(own_gram, 3 - side, 3, 0) * theirs)
    squares = jnp.full((8, 128), squares, f32)
    squares = squares + swap_tp(squares, 1)
    across, base_tile, squares = lax.optimization_barrier((across, base_tile, squares))
    across_partner = swap_tp(across, 1)
    squares = squares + swap_tp(squares, 2)
    scale = (inner_rate / jnp.sqrt(squares[0, :1] / entries + 1e-06))

    pieces = (out_grad, partner, across, across_partner)
    scale, base_tile = lax.optimization_barrier((scale, base_tile))
    sends = pseudo_gradient(FIRST + LATER, "pseudo_gradient", at, scale, ct, pieces, drift)
    waves, later = sends[:4], sends[4:]
    here, there = pass_on(waves[:2], later[:3], "x"), pass_on(waves[2:], later[3:], "y")
    there, base_tile = lax.optimization_barrier((there, base_tile))
    base_tiles = jnp.stack([base_tile, move(base_tile, "z", 1)])
    here, there = arrive(later[0], *here, "x"), arrive(later[3], *there, "y")
    here, there = lax.optimization_barrier((here, there))
    here, there = reduce_tiles(here, "y"), reduce_tiles(there, "x")
    here, there = lax.reduce_precision(here, 8, 7), lax.reduce_precision(there, 8, 7)
    crossed = move(jnp.stack([there, here]).astype(bf16), "z", 1)
    means = (jnp.stack([here, there]) + crossed.astype(f32)) / lax.axis_size("worker")
    fresh = (base_tiles - (outer_rate * (1.0 + outer_mu)) * means).astype(bf16)
    mean, tile, opposite = means[0], fresh[0], fresh[1]

    def mean_rows(k):
        return lax.dynamic_slice_in_dim(mean, ((x + k) % NX) * own_rows, own_rows, 0)

    here_got = ring([tile] * 3, "y", -1)
    there_got = ring(
        [jnp.concatenate([opposite, mean_rows(NX - k).astype(bf16)]) for k in (1, 2, 3)], "x", -1
    )
    means = jnp.stack([mean_rows(0)] + [got[TILE_R:].astype(f32) for got in there_got])
    there_got = [got[:TILE_R] for got in there_got]
    here = jnp.stack([tile] + here_got)
    there = jnp.stack([opposite] + there_got)
    here_1, here_3 = move(here, "x", -1), move(here, "x", 1)
    there_1, there_3 = move(there, "y", -1), move(there, "y", 1)
    last = [
        move(here_1[:2], "x", -1), move(here_3[2:], "x", 1),
        move(there_1[:2], "y", -1), move(there_3[2:], "y", 1),
    ]
    new_master, new_momentum = outer_rows(at, master, momentum, means)
    rows, width = drift.shape[1], drift.shape[2]
    so_far = place(
        "place_first",
        [[(0, n, k) for n in range(4)] for k in (0, 1, 3)] + [[(1, ky, n) for n in range(4)] for ky in (0, 1, 3)],
        at, [here, here_1, here_3, there, there_1, there_3], rows, width,
    )
    new_params = place(
        "place_last",
        [[(0, 0, 2), (0, 1, 2)], [(0, 2, 2), (0, 3, 2)], [(1, 2, 0), (1, 2, 1)], [(1, 2, 2), (1, 2, 3)]],
        at, last, rows, width, so_far,
    )
    return (new_params, new_master, new_momentum)


def solution(mesh):
    placed = (
        P("worker", "tp"),
        P("worker", "tp"),
        P("worker", "tp"),
        P("worker", "tp"),
        P("worker"),
        P("worker", "tp", None),
        P(("tp", "worker"), None),
        P(("tp", "worker"), None),
    )
    return jax.shard_map(
        per_device,
        mesh=mesh,
        in_specs=placed,
        out_specs=(P("tp", None), P(("tp", "worker"), None), P(("tp", "worker"), None)),
        check_vma=False,
    )
```

```python
import functools
import math

import jax
import jax.numpy as jnp
from jax import lax
from jax.experimental import pallas as pl
from jax.experimental.pallas import tpu as pltpu
from jax.sharding import PartitionSpec as P

HD = 128
NX, NY, NZ = 4, 4, 2
TILE_R = 80
HALF_C = 640

inner_rate = 0.8
outer_rate = 0.7
outer_mu = 0.9
neg_big = -1e30
bf16 = jnp.bfloat16
f32 = jnp.float32
VMEM_LIMIT = 60 << 20


def worker_of(zh, y, x):
    return (zh % NZ) * NX * NY + (y % NY) * NX + (x % NX)


def move(value, axis, step):
    pairs = []
    for zh in range(NZ):
        for y in range(NY):
            for x in range(NX):
                to = {
                    "x": worker_of(zh, y, x + step),
                    "y": worker_of(zh, y + step, x),
                    "z": worker_of(zh + step, y, x),
                }[axis]
                pairs.append((worker_of(zh, y, x), to))
    return lax.ppermute(value, "worker", pairs)


def swap_tp(value, bit):
    return lax.ppermute(value, "tp", [(t, t ^ bit) for t in range(4)])


LOWER = [(i, j) for i in range(3) for j in range(i + 1)]


def cotangent_gram_body(grad_ref, gram_ref):
    for n, (i, j) in enumerate(LOWER):
        gram_ref[n] = lax.dot_general(
            grad_ref[i * HD:(i + 1) * HD, :], grad_ref[j * HD:(j + 1) * HD, :],
            (((1,), (1,)), ((), ())), preferred_element_type=f32,
        )


def cotangent_gram(grad):
    return pl.pallas_call(
        cotangent_gram_body,
        out_shape=jax.ShapeDtypeStruct((len(LOWER), HD, HD), f32),
        name="cotangent_gram",
    )(grad)


def attention_body(q_ref, k_ref, v_ref, seg_row_ref, ct_ref, gram_ref):
    tokens, width = q_ref.shape
    scale = 1.0 / math.sqrt(HD)
    blocks = tokens // HD
    seg_row = seg_row_ref[...]
    seg_col = jnp.broadcast_to(seg_row.astype(f32), (HD, tokens)).T.astype(jnp.int32)
    for h in range(width // HD):
        cols = slice(h * HD, (h + 1) * HD)
        for b in range(blocks):
            queries = slice(b * HD, (b + 1) * HD)
            seen = (b + 1) * HD
            scores = lax.dot_general(
                k_ref[:seen, cols], q_ref[queries, cols], (((1,), (1,)), ((), ())),
                preferred_element_type=f32,
            ) * scale
            key_at = lax.broadcasted_iota(jnp.int32, (seen, HD), 0)
            query_at = lax.broadcasted_iota(jnp.int32, (seen, HD), 1) + b * HD
            allowed = (key_at <= query_at) & (seg_col[:seen, :] == seg_row[:, queries])
            scores = jnp.where(allowed, scores, neg_big)
            exp_scores = jnp.exp(scores - jnp.max(scores, axis=0, keepdims=True))
            total = jnp.sum(exp_scores, axis=0, keepdims=True)
            weights = (exp_scores * (1.0 / total)).astype(bf16)
            ct_ref[cols, queries] = lax.dot_general(
                v_ref[:seen, cols], weights, (((0,), (0,)), ((), ())),
                preferred_element_type=f32,
            ).astype(bf16)
    for n, (i, j) in enumerate(LOWER):
        block = lax.dot_general(
            ct_ref[:, i * HD:(i + 1) * HD], ct_ref[:, j * HD:(j + 1) * HD],
            (((0,), (0,)), ((), ())), preferred_element_type=f32,
        )
        gram_ref[n] = block if i == j else 2.0 * block


def attention(queries, keys, values, segments):
    tokens, width = queries.shape
    return pl.pallas_call(
        attention_body,
        out_shape=(
            jax.ShapeDtypeStruct((width, tokens), bf16),
            jax.ShapeDtypeStruct((len(LOWER), HD, HD), f32),
        ),
        compiler_params=pltpu.CompilerParams(vmem_limit_bytes=VMEM_LIMIT),
        name="attention",
    )(queries, keys, values, segments.reshape(1, tokens))


def column_of(tp, half, quarter):
    first = (tp ^ (2 * half) ^ (quarter // 2)) * (2 * HALF_C) + (quarter % 2) * HALF_C
    return pl.multiple_of(first, HALF_C)


def row_of(zh, y, j, ky):
    return pl.multiple_of((zh ^ j) * (NY * TILE_R) + ((y + ky) % NY) * TILE_R, TILE_R)


K_ORDER = (2, 1, 3, 0)
UP_DOWN = ((2, 2, 1, 1), (3, 3, 2, 2))
FIRST = [[(0, n, far[n]) for n in range(4)] for far in UP_DOWN] + [
    [(1, far[n], n) for n in range(4)] for far in UP_DOWN
]
LATER = [
    [(0, n, 0) for n in range(4)], [(0, 0, 1), (0, 1, 1)], [(0, 2, 3), (0, 3, 3)],
    [(1, 0, n) for n in range(4)], [(1, 1, 0), (1, 1, 1)], [(1, 3, 2), (1, 3, 3)],
]


def pseudo_body(outputs, at_ref, scale_ref, ct_ref, g0_ref, g1_ref, g2_ref, g3_ref, drift_ref, *rest):
    outs = rest[:len(outputs)]
    drift_buf, g_buf, rows_buf, out_buf, drift_sems, g_sems, out_sems = rest[len(outputs):]
    x, y, zh, tp = at_ref[0], at_ref[1], at_ref[2], at_ref[3]
    scale = scale_ref[0]
    pieces = ((g0_ref, g1_ref), (g2_ref, g3_ref))

    def g_copy(slot, ref, k):
        return pltpu.make_async_copy(
            ref.at[:, pl.ds(pl.multiple_of(((x + k) % 2) * HALF_C, HALF_C), HALF_C)],
            g_buf.at[slot], g_sems.at[slot],
        )

    def g_start(slot, ref, k):
        g_copy(slot, ref, k).start()

    def drift_copy(slot, k, half):
        return pltpu.make_async_copy(
            drift_ref.at[0, :, pl.ds(column_of(tp, half, (x + k) % NX), HALF_C)],
            drift_buf.at[slot], drift_sems.at[slot],
        )

    steps = [(k, half) for k in K_ORDER for half in range(2)]
    for slot, (k, half) in enumerate(steps):
        for side, ref in enumerate(pieces[half]):
            pl.when(((x + k) % NX) // 2 == side)(functools.partial(g_start, slot, ref, k))
        drift_copy(slot, k, half).start()
    for j in range(2):
        for ky in range(NY):
            first = (j * NY + ky) * TILE_R
            rows_buf[first:first + TILE_R, :] = ct_ref[pl.ds(row_of(zh, y, j, ky), TILE_R), :]

    copies = []
    for slot, (k, half) in enumerate(steps):
        cols = slice(half * HALF_C, (half + 1) * HALF_C)
        g_copy(slot, g0_ref, k).wait()
        drift_copy(slot, k, half).wait()
        for j in range(2):
            rows = slice(j * NY * TILE_R, (j + 1) * NY * TILE_R)
            block = jnp.dot(rows_buf[rows, :], g_buf[slot], preferred_element_type=f32)
            for ky in range(NY):
                own = drift_buf[slot, pl.ds(row_of(zh, y, j, ky), TILE_R), :]
                value = block[ky * TILE_R:(ky + 1) * TILE_R] * scale + own.astype(f32)
                out_buf[k, j * NY + ky, :, cols] = value.astype(bf16)
        if half == 1:
            for j in range(2):
                for ky in range(NY):
                    o, index = next(
                        (o, tiles.index((j, ky, k))) for o, tiles in enumerate(outputs) if (j, ky, k) in tiles
                    )
                    copies.append(pltpu.make_async_copy(
                        out_buf.at[k, j * NY + ky], outs[o].at[index], out_sems.at[len(copies)]
                    ))
                    copies[-1].start()
    for one in copies:
        one.wait()


def pseudo_gradient(outputs, name, at, scale, ct, pieces, drift):
    smem = pl.BlockSpec(memory_space=pltpu.SMEM)
    hbm = pl.BlockSpec(memory_space=pl.ANY)
    tokens, rows = ct.shape[1], ct.shape[0]
    count = sum(len(tiles) for tiles in outputs)
    return pl.pallas_call(
        functools.partial(pseudo_body, outputs),
        out_shape=tuple(
            jax.ShapeDtypeStruct((len(tiles), TILE_R, 2 * HALF_C), bf16) for tiles in outputs
        ),
        in_specs=[smem, smem, pl.BlockSpec(memory_space=pltpu.VMEM)] + [hbm] * 5,
        out_specs=(hbm,) * len(outputs),
        scratch_shapes=[
            pltpu.VMEM((8, rows, HALF_C), bf16),
            pltpu.VMEM((8, tokens, HALF_C), bf16),
            pltpu.VMEM(ct.shape, bf16),
            pltpu.VMEM((NX, 2 * NY, TILE_R, 2 * HALF_C), bf16),
            pltpu.SemaphoreType.DMA((8,)),
            pltpu.SemaphoreType.DMA((8,)),
            pltpu.SemaphoreType.DMA((count,)),
        ],
        compiler_params=pltpu.CompilerParams(vmem_limit_bytes=VMEM_LIMIT),
        cost_estimate=pl.CostEstimate(
            flops=2 * rows * tokens * 5120, bytes_accessed=18_000_000, transcendentals=0
        ),
        name=name,
    )(at, scale, ct, *pieces, drift)


def base_body(at_ref, master_ref, momentum_ref, base_ref):
    tp = at_ref[3]
    for quarter in range(NX):
        for half in range(2):
            cols = pl.ds(column_of(tp, half, quarter), HALF_C)
            base_ref[quarter, :, half * HALF_C:(half + 1) * HALF_C] = (
                master_ref[:, cols] - (outer_rate * outer_mu * outer_mu) * momentum_ref[:, cols]
            )


def base_rows(at, master, momentum):
    vmem = pl.BlockSpec(memory_space=pltpu.VMEM)
    return pl.pallas_call(
        base_body,
        out_shape=jax.ShapeDtypeStruct((NX, master.shape[0], 2 * HALF_C), f32),
        in_specs=[pl.BlockSpec(memory_space=pltpu.SMEM), vmem, vmem],
        out_specs=vmem,
        name="base_rows",
    )(at, master, momentum)


def outer_body(at_ref, master_ref, momentum_ref, mean_ref, new_master_ref, new_momentum_ref):
    x, tp = at_ref[0], at_ref[3]
    for quarter in range(NX):
        for half in range(2):
            cols = pl.ds(column_of(tp, half, quarter), HALF_C)
            mean = mean_ref[(quarter - x + NX) % NX, :, half * HALF_C:(half + 1) * HALF_C]
            new = outer_mu * momentum_ref[:, cols] + mean
            new_momentum_ref[:, cols] = new
            new_master_ref[:, cols] = master_ref[:, cols] - outer_rate * (mean + outer_mu * new)


def outer_rows(at, master, momentum, mean):
    vmem = pl.BlockSpec(memory_space=pltpu.VMEM)
    out = jax.ShapeDtypeStruct(master.shape, f32)
    return pl.pallas_call(
        outer_body,
        out_shape=(out, out),
        in_specs=[pl.BlockSpec(memory_space=pltpu.SMEM), vmem, vmem, vmem],
        out_specs=(vmem, vmem),
        name="outer_rows",
    )(at, master, momentum, mean)


def place_body(where, at_ref, *rest):
    count = len(where)
    blocks, (out_ref, stage, in_sems, out_sems) = rest[:count], rest[-4:]
    x, y, zh, tp = at_ref[0], at_ref[1], at_ref[2], at_ref[3]
    slots = [sum(len(tiles) for tiles in where[:n]) for n in range(count)]
    loads = [
        pltpu.make_async_copy(blocks[n], stage.at[slots[n]:slots[n] + len(where[n])], in_sems.at[n])
        for n in range(count)
    ]
    for one in loads:
        one.start()
    stores = []
    for n, tiles in enumerate(where):
        loads[n].wait()
        for m, (j, ky, k) in enumerate(tiles):
            for half in range(2):
                stores.append(pltpu.make_async_copy(
                    stage.at[slots[n] + m, :, half * HALF_C:(half + 1) * HALF_C],
                    out_ref.at[pl.ds(row_of(zh, y, j, ky), TILE_R),
                               pl.ds(column_of(tp, half, (x + k) % NX), HALF_C)],
                    out_sems.at[len(stores)],
                ))
                stores[-1].start()
    for one in stores:
        one.wait()


def place(name, where, at, blocks, rows, width, so_far=None):
    hbm = pl.BlockSpec(memory_space=pl.ANY)
    count = sum(len(tiles) for tiles in where)
    operands = [at, *blocks] + ([] if so_far is None else [so_far])
    return pl.pallas_call(
        functools.partial(place_body, where),
        out_shape=jax.ShapeDtypeStruct((rows, width), bf16),
        in_specs=[pl.BlockSpec(memory_space=pltpu.SMEM)] + [hbm] * (len(operands) - 1),
        out_specs=hbm,
        scratch_shapes=[
            pltpu.VMEM((count, TILE_R, 2 * HALF_C), bf16),
            pltpu.SemaphoreType.DMA((len(where),)),
            pltpu.SemaphoreType.DMA((2 * count,)),
        ],
        input_output_aliases={} if so_far is None else {len(operands) - 1: 0},
        compiler_params=pltpu.CompilerParams(vmem_limit_bytes=VMEM_LIMIT),
        cost_estimate=pl.CostEstimate(
            flops=0, bytes_accessed=4 * count * TILE_R * 2 * HALF_C, transcendentals=0
        ),
        name=name,
    )(*operands)


def add(*terms):
    total = terms[0].astype(f32)
    for term in terms[1:]:
        total = total + term.astype(f32)
    return total


def ring(values, axis, sign):
    two = move(values[1], axis, 2 * sign)
    one = move(values[0], axis, sign)
    three = move(values[2], axis, -sign)
    return [one, two, three]


def pass_on(waves, later, axis):
    up, down = move(waves[0], axis, 1), move(waves[1], axis, -1)
    onward_up = add(later[1], up[:2]).astype(bf16)
    onward_down = add(later[2], down[2:]).astype(bf16)
    return up, down, onward_up, onward_down


def arrive(own, up, down, onward_up, onward_down, axis):
    last_up, last_down = move(onward_up, axis, 1), move(onward_down, axis, -1)
    low = add(own[:2], down[:2], last_up)
    high = add(own[2:], up[2:], last_down)
    return jnp.concatenate([low, high])


def reduce_tiles(tiles, axis):
    sent = tiles.astype(bf16)
    return add(tiles[0], *ring([sent[1], sent[2], sent[3]], axis, 1))


def per_device(queries, keys, values, out_grad, segments, drift, master, momentum):
    tp = lax.axis_index("tp")
    worker = lax.axis_index("worker")
    x, y, zh = worker % NX, (worker // NX) % NY, worker // (NX * NY)
    at = jnp.stack([x, y, zh, tp]).astype(jnp.int32)
    own_rows = master.shape[0]
    entries = queries.shape[1] * lax.axis_size("tp") * drift.shape[2]

    partner = swap_tp(out_grad, 1)

    gram = cotangent_gram(out_grad)
    far = swap_tp(gram, 2)

    gram, queries = lax.optimization_barrier((gram, queries))
    ct, own_gram = attention(queries, keys, values, segments)
    ct, early_at, crossing = lax.optimization_barrier((ct, at, out_grad))
    across = swap_tp(crossing, 2)
    base = base_rows(early_at, master, momentum)
    rings = [[first + n for n in range(NX)] for first in range(0, NX * NY * NZ, NX)]
    base_tile = lax.all_to_all(base, "worker", 0, 0, axis_index_groups=rings)
    base_tile = base_tile.reshape(TILE_R, 2 * HALF_C)
    far, gram, ct, own_gram = lax.optimization_barrier((far, gram, ct, own_gram))
    gram = gram + far
    squares = jnp.sum(own_gram * (gram + swap_tp(gram, 1)))
    squares = jnp.full((8, 128), squares, f32)
    squares = squares + swap_tp(squares, 1)
    across, base_tile, squares = lax.optimization_barrier((across, base_tile, squares))
    across_partner = swap_tp(across, 1)
    squares = squares + swap_tp(squares, 2)
    scale = (inner_rate / jnp.sqrt(squares[0, :1] / entries + 1e-06))

    pieces = (out_grad, partner, across, across_partner)
    scale, base_tile = lax.optimization_barrier((scale, base_tile))
    sends = pseudo_gradient(FIRST + LATER, "pseudo_gradient", at, scale, ct, pieces, drift)
    waves, later = sends[:4], sends[4:]
    here, there = pass_on(waves[:2], later[:3], "x"), pass_on(waves[2:], later[3:], "y")
    there, base_tile = lax.optimization_barrier((there, base_tile))
    base_tiles = jnp.stack([base_tile, move(base_tile, "z", 1)])
    here, there = arrive(later[0], *here, "x"), arrive(later[3], *there, "y")
    here, there = lax.optimization_barrier((here, there))
    here, there = reduce_tiles(here, "y"), reduce_tiles(there, "x")
    here, there = lax.reduce_precision(here, 8, 7), lax.reduce_precision(there, 8, 7)
    crossed = move(jnp.stack([there, here]).astype(bf16), "z", 1)
    means = (jnp.stack([here, there]) + crossed.astype(f32)) / lax.axis_size("worker")
    fresh = (base_tiles - (outer_rate * (1.0 + outer_mu)) * means).astype(bf16)
    mean, tile, opposite = means[0], fresh[0], fresh[1]

    def mean_rows(k):
        return lax.dynamic_slice_in_dim(mean, ((x + k) % NX) * own_rows, own_rows, 0)

    there_got = ring(
        [jnp.concatenate([opposite, mean_rows(NX - k).astype(bf16)]) for k in (1, 2, 3)], "x", -1
    )
    here_got = ring([tile] * 3, "y", -1)
    means = jnp.stack([mean_rows(0)] + [got[TILE_R:].astype(f32) for got in there_got])
    there_got = [got[:TILE_R] for got in there_got]
    here = jnp.stack([tile] + here_got)
    there = jnp.stack([opposite] + there_got)
    here_1, here_3 = move(here, "x", -1), move(here, "x", 1)
    there_1, there_3 = move(there, "y", -1), move(there, "y", 1)
    last = [
        move(here_1[:2], "x", -1), move(here_3[2:], "x", 1),
        move(there_1[:2], "y", -1), move(there_3[2:], "y", 1),
    ]
    new_master, new_momentum = outer_rows(at, master, momentum, means)
    rows, width = drift.shape[1], drift.shape[2]
    so_far = place(
        "place_first",
        [[(0, n, k) for n in range(4)] for k in (0, 1, 3)] + [[(1, ky, n) for n in range(4)] for ky in (0, 1, 3)],
        at, [here, here_1, here_3, there, there_1, there_3], rows, width,
    )
    new_params = place(
        "place_last",
        [[(0, 0, 2), (0, 1, 2)], [(0, 2, 2), (0, 3, 2)], [(1, 2, 0), (1, 2, 1)], [(1, 2, 2), (1, 2, 3)]],
        at, last, rows, width, so_far,
    )
    return (new_params, new_master, new_momentum)


def solution(mesh):
    placed = (
        P("worker", "tp"),
        P("worker", "tp"),
        P("worker", "tp"),
        P("worker", "tp"),
        P("worker"),
        P("worker", "tp", None),
        P(("tp", "worker"), None),
        P(("tp", "worker"), None),
    )
    return jax.shard_map(
        per_device,
        mesh=mesh,
        in_specs=placed,
        out_specs=(P("tp", None), P(("tp", "worker"), None), P(("tp", "worker"), None)),
        check_vma=False,
    )
```

```python
import functools
import math

import jax
import jax.numpy as jnp
from jax import lax
from jax.experimental import pallas as pl
from jax.experimental.pallas import tpu as pltpu
from jax.sharding import PartitionSpec as P

HD = 128
NX, NY, NZ = 4, 4, 2
TILE_R = 80
HALF_C = 640

inner_rate = 0.8
outer_rate = 0.7
outer_mu = 0.9
neg_big = -1e30
bf16 = jnp.bfloat16
f32 = jnp.float32
VMEM_LIMIT = 60 << 20


def worker_of(zh, y, x):
    return (zh % NZ) * NX * NY + (y % NY) * NX + (x % NX)


def move(value, axis, step):
    pairs = []
    for zh in range(NZ):
        for y in range(NY):
            for x in range(NX):
                to = {
                    "x": worker_of(zh, y, x + step),
                    "y": worker_of(zh, y + step, x),
                    "z": worker_of(zh + step, y, x),
                }[axis]
                pairs.append((worker_of(zh, y, x), to))
    return lax.ppermute(value, "worker", pairs)


def swap_tp(value, bit):
    return lax.ppermute(value, "tp", [(t, t ^ bit) for t in range(4)])


LOWER = [(i, j) for i in range(3) for j in range(i + 1)]


def cotangent_gram_body(grad_ref, gram_ref):
    for n, (i, j) in enumerate(LOWER):
        gram_ref[n] = lax.dot_general(
            grad_ref[i * HD:(i + 1) * HD, :], grad_ref[j * HD:(j + 1) * HD, :],
            (((1,), (1,)), ((), ())), preferred_element_type=f32,
        )


def cotangent_gram(grad):
    return pl.pallas_call(
        cotangent_gram_body,
        out_shape=jax.ShapeDtypeStruct((len(LOWER), HD, HD), f32),
        name="cotangent_gram",
    )(grad)


def attention_body(q_ref, k_ref, v_ref, seg_row_ref, ct_ref, gram_ref):
    tokens, width = q_ref.shape
    scale = 1.0 / math.sqrt(HD)
    blocks = tokens // HD
    seg_row = seg_row_ref[...]
    seg_col = jnp.broadcast_to(seg_row.astype(f32), (HD, tokens)).T.astype(jnp.int32)
    for h in range(width // HD):
        cols = slice(h * HD, (h + 1) * HD)
        for b in range(blocks):
            queries = slice(b * HD, (b + 1) * HD)
            seen = (b + 1) * HD
            scores = lax.dot_general(
                k_ref[:seen, cols], q_ref[queries, cols], (((1,), (1,)), ((), ())),
                preferred_element_type=f32,
            ) * scale
            key_at = lax.broadcasted_iota(jnp.int32, (seen, HD), 0)
            query_at = lax.broadcasted_iota(jnp.int32, (seen, HD), 1) + b * HD
            allowed = (key_at <= query_at) & (seg_col[:seen, :] == seg_row[:, queries])
            scores = jnp.where(allowed, scores, neg_big)
            exp_scores = jnp.exp(scores - jnp.max(scores, axis=0, keepdims=True))
            total = jnp.sum(exp_scores, axis=0, keepdims=True)
            weights = (exp_scores * (1.0 / total)).astype(bf16)
            ct_ref[cols, queries] = lax.dot_general(
                v_ref[:seen, cols], weights, (((0,), (0,)), ((), ())),
                preferred_element_type=f32,
            ).astype(bf16)
    for n, (i, j) in enumerate(LOWER):
        block = lax.dot_general(
            ct_ref[:, i * HD:(i + 1) * HD], ct_ref[:, j * HD:(j + 1) * HD],
            (((0,), (0,)), ((), ())), preferred_element_type=f32,
        )
        gram_ref[n] = block if i == j else 2.0 * block


def attention(queries, keys, values, segments):
    tokens, width = queries.shape
    return pl.pallas_call(
        attention_body,
        out_shape=(
            jax.ShapeDtypeStruct((width, tokens), bf16),
            jax.ShapeDtypeStruct((len(LOWER), HD, HD), f32),
        ),
        compiler_params=pltpu.CompilerParams(vmem_limit_bytes=VMEM_LIMIT),
        name="attention",
    )(queries, keys, values, segments.reshape(1, tokens))


def column_of(tp, half, quarter):
    first = (tp ^ (2 * half) ^ (quarter // 2)) * (2 * HALF_C) + (quarter % 2) * HALF_C
    return pl.multiple_of(first, HALF_C)


def row_of(zh, y, j, ky):
    return pl.multiple_of((zh ^ j) * (NY * TILE_R) + ((y + ky) % NY) * TILE_R, TILE_R)


K_ORDER = (2, 1, 3, 0)
UP_DOWN = ((2, 2, 1, 1), (3, 3, 2, 2))
FIRST = [[(0, n, far[n]) for n in range(4)] for far in UP_DOWN] + [
    [(1, far[n], n) for n in range(4)] for far in UP_DOWN
]
LATER = [
    [(0, n, 0) for n in range(4)], [(0, 0, 1), (0, 1, 1)], [(0, 2, 3), (0, 3, 3)],
    [(1, 0, n) for n in range(4)], [(1, 1, 0), (1, 1, 1)], [(1, 3, 2), (1, 3, 3)],
]


def pseudo_body(outputs, at_ref, scale_ref, ct_ref, g0_ref, g1_ref, g2_ref, g3_ref, drift_ref, *rest):
    outs = rest[:len(outputs)]
    drift_buf, g_buf, rows_buf, out_buf, drift_sems, g_sems, out_sems = rest[len(outputs):]
    x, y, zh, tp = at_ref[0], at_ref[1], at_ref[2], at_ref[3]
    scale = scale_ref[0]
    pieces = ((g0_ref, g1_ref), (g2_ref, g3_ref))

    def g_copy(slot, ref, k):
        return pltpu.make_async_copy(
            ref.at[:, pl.ds(pl.multiple_of(((x + k) % 2) * HALF_C, HALF_C), HALF_C)],
            g_buf.at[slot], g_sems.at[slot],
        )

    def g_start(slot, ref, k):
        g_copy(slot, ref, k).start()

    def drift_copy(slot, k, half):
        return pltpu.make_async_copy(
            drift_ref.at[0, :, pl.ds(column_of(tp, half, (x + k) % NX), HALF_C)],
            drift_buf.at[slot], drift_sems.at[slot],
        )

    steps = [(k, half) for k in K_ORDER for half in range(2)]
    for slot, (k, half) in enumerate(steps):
        for side, ref in enumerate(pieces[half]):
            pl.when(((x + k) % NX) // 2 == side)(functools.partial(g_start, slot, ref, k))
        drift_copy(slot, k, half).start()
    for j in range(2):
        for ky in range(NY):
            first = (j * NY + ky) * TILE_R
            rows_buf[first:first + TILE_R, :] = ct_ref[pl.ds(row_of(zh, y, j, ky), TILE_R), :]

    copies = []
    for slot, (k, half) in enumerate(steps):
        cols = slice(half * HALF_C, (half + 1) * HALF_C)
        g_copy(slot, g0_ref, k).wait()
        drift_copy(slot, k, half).wait()
        for j in range(2):
            rows = slice(j * NY * TILE_R, (j + 1) * NY * TILE_R)
            block = jnp.dot(rows_buf[rows, :], g_buf[slot], preferred_element_type=f32)
            for ky in range(NY):
                own = drift_buf[slot, pl.ds(row_of(zh, y, j, ky), TILE_R), :]
                value = block[ky * TILE_R:(ky + 1) * TILE_R] * scale + own.astype(f32)
                out_buf[k, j * NY + ky, :, cols] = value.astype(bf16)
        if half == 1:
            for j in range(2):
                for ky in range(NY):
                    o, index = next(
                        (o, tiles.index((j, ky, k))) for o, tiles in enumerate(outputs) if (j, ky, k) in tiles
                    )
                    copies.append(pltpu.make_async_copy(
                        out_buf.at[k, j * NY + ky], outs[o].at[index], out_sems.at[len(copies)]
                    ))
                    copies[-1].start()
    for one in copies:
        one.wait()


def pseudo_gradient(outputs, name, at, scale, ct, pieces, drift):
    smem = pl.BlockSpec(memory_space=pltpu.SMEM)
    hbm = pl.BlockSpec(memory_space=pl.ANY)
    tokens, rows = ct.shape[1], ct.shape[0]
    count = sum(len(tiles) for tiles in outputs)
    return pl.pallas_call(
        functools.partial(pseudo_body, outputs),
        out_shape=tuple(
            jax.ShapeDtypeStruct((len(tiles), TILE_R, 2 * HALF_C), bf16) for tiles in outputs
        ),
        in_specs=[smem, smem, pl.BlockSpec(memory_space=pltpu.VMEM)] + [hbm] * 5,
        out_specs=(hbm,) * len(outputs),
        scratch_shapes=[
            pltpu.VMEM((8, rows, HALF_C), bf16),
            pltpu.VMEM((8, tokens, HALF_C), bf16),
            pltpu.VMEM(ct.shape, bf16),
            pltpu.VMEM((NX, 2 * NY, TILE_R, 2 * HALF_C), bf16),
            pltpu.SemaphoreType.DMA((8,)),
            pltpu.SemaphoreType.DMA((8,)),
            pltpu.SemaphoreType.DMA((count,)),
        ],
        compiler_params=pltpu.CompilerParams(vmem_limit_bytes=VMEM_LIMIT),
        cost_estimate=pl.CostEstimate(
            flops=2 * rows * tokens * 5120, bytes_accessed=18_000_000, transcendentals=0
        ),
        name=name,
    )(at, scale, ct, *pieces, drift)


def base_body(at_ref, master_ref, momentum_ref, base_ref):
    tp = at_ref[3]
    for quarter in range(NX):
        for half in range(2):
            cols = pl.ds(column_of(tp, half, quarter), HALF_C)
            base_ref[quarter, :, half * HALF_C:(half + 1) * HALF_C] = (
                master_ref[:, cols] - (outer_rate * outer_mu * outer_mu) * momentum_ref[:, cols]
            )


def base_rows(at, master, momentum):
    vmem = pl.BlockSpec(memory_space=pltpu.VMEM)
    return pl.pallas_call(
        base_body,
        out_shape=jax.ShapeDtypeStruct((NX, master.shape[0], 2 * HALF_C), f32),
        in_specs=[pl.BlockSpec(memory_space=pltpu.SMEM), vmem, vmem],
        out_specs=vmem,
        name="base_rows",
    )(at, master, momentum)


def outer_body(at_ref, master_ref, momentum_ref, mean_ref, new_master_ref, new_momentum_ref):
    x, tp = at_ref[0], at_ref[3]
    for quarter in range(NX):
        for half in range(2):
            cols = pl.ds(column_of(tp, half, quarter), HALF_C)
            mean = mean_ref[(quarter - x + NX) % NX, :, half * HALF_C:(half + 1) * HALF_C]
            new = outer_mu * momentum_ref[:, cols] + mean
            new_momentum_ref[:, cols] = new
            new_master_ref[:, cols] = master_ref[:, cols] - outer_rate * (mean + outer_mu * new)


def outer_rows(at, master, momentum, mean):
    vmem = pl.BlockSpec(memory_space=pltpu.VMEM)
    out = jax.ShapeDtypeStruct(master.shape, f32)
    return pl.pallas_call(
        outer_body,
        out_shape=(out, out),
        in_specs=[pl.BlockSpec(memory_space=pltpu.SMEM), vmem, vmem, vmem],
        out_specs=(vmem, vmem),
        name="outer_rows",
    )(at, master, momentum, mean)


def place_body(where, at_ref, *rest):
    count = len(where)
    blocks, (out_ref, stage, in_sems, out_sems) = rest[:count], rest[-4:]
    x, y, zh, tp = at_ref[0], at_ref[1], at_ref[2], at_ref[3]
    slots = [sum(len(tiles) for tiles in where[:n]) for n in range(count)]
    loads = [
        pltpu.make_async_copy(blocks[n], stage.at[slots[n]:slots[n] + len(where[n])], in_sems.at[n])
        for n in range(count)
    ]
    for one in loads:
        one.start()
    stores = []
    for n, tiles in enumerate(where):
        loads[n].wait()
        for m, (j, ky, k) in enumerate(tiles):
            for half in range(2):
                stores.append(pltpu.make_async_copy(
                    stage.at[slots[n] + m, :, half * HALF_C:(half + 1) * HALF_C],
                    out_ref.at[pl.ds(row_of(zh, y, j, ky), TILE_R),
                               pl.ds(column_of(tp, half, (x + k) % NX), HALF_C)],
                    out_sems.at[len(stores)],
                ))
                stores[-1].start()
    for one in stores:
        one.wait()


def place(name, where, at, blocks, rows, width, so_far=None):
    hbm = pl.BlockSpec(memory_space=pl.ANY)
    count = sum(len(tiles) for tiles in where)
    operands = [at, *blocks] + ([] if so_far is None else [so_far])
    return pl.pallas_call(
        functools.partial(place_body, where),
        out_shape=jax.ShapeDtypeStruct((rows, width), bf16),
        in_specs=[pl.BlockSpec(memory_space=pltpu.SMEM)] + [hbm] * (len(operands) - 1),
        out_specs=hbm,
        scratch_shapes=[
            pltpu.VMEM((count, TILE_R, 2 * HALF_C), bf16),
            pltpu.SemaphoreType.DMA((len(where),)),
            pltpu.SemaphoreType.DMA((2 * count,)),
        ],
        input_output_aliases={} if so_far is None else {len(operands) - 1: 0},
        compiler_params=pltpu.CompilerParams(vmem_limit_bytes=VMEM_LIMIT),
        cost_estimate=pl.CostEstimate(
            flops=0, bytes_accessed=4 * count * TILE_R * 2 * HALF_C, transcendentals=0
        ),
        name=name,
    )(*operands)


def add(*terms):
    total = terms[0].astype(f32)
    for term in terms[1:]:
        total = total + term.astype(f32)
    return total


def ring(values, axis, sign):
    two = move(values[1], axis, 2 * sign)
    one = move(values[0], axis, sign)
    three = move(values[2], axis, -sign)
    return [one, two, three]


def pass_on(waves, later, axis):
    up, down = move(waves[0], axis, 1), move(waves[1], axis, -1)
    onward_up = add(later[1], up[:2]).astype(bf16)
    onward_down = add(later[2], down[2:]).astype(bf16)
    return up, down, onward_up, onward_down


def arrive(own, up, down, onward_up, onward_down, axis):
    last_up, last_down = move(onward_up, axis, 1), move(onward_down, axis, -1)
    low = add(own[:2], down[:2], last_up)
    high = add(own[2:], up[2:], last_down)
    return jnp.concatenate([low, high])


def reduce_tiles(tiles, axis):
    sent = tiles.astype(bf16)
    return add(tiles[0], *ring([sent[1], sent[2], sent[3]], axis, 1))


def per_device(queries, keys, values, out_grad, segments, drift, master, momentum):
    tp = lax.axis_index("tp")
    worker = lax.axis_index("worker")
    x, y, zh = worker % NX, (worker // NX) % NY, worker // (NX * NY)
    at = jnp.stack([x, y, zh, tp]).astype(jnp.int32)
    own_rows = master.shape[0]
    entries = queries.shape[1] * lax.axis_size("tp") * drift.shape[2]

    partner = swap_tp(out_grad, 1)

    gram = cotangent_gram(out_grad)
    far = swap_tp(gram, 2)

    gram, queries = lax.optimization_barrier((gram, queries))
    ct, own_gram = attention(queries, keys, values, segments)
    ct, early_at, crossing = lax.optimization_barrier((ct, at, out_grad))
    across = swap_tp(crossing, 2)
    base = base_rows(early_at, master, momentum)
    rings = [[first + n for n in range(NX)] for first in range(0, NX * NY * NZ, NX)]
    base_tile = lax.all_to_all(base, "worker", 0, 0, axis_index_groups=rings)
    base_tile = base_tile.reshape(TILE_R, 2 * HALF_C)
    far, gram, ct, own_gram = lax.optimization_barrier((far, gram, ct, own_gram))
    gram = gram + far
    squares = jnp.sum(own_gram * (gram + swap_tp(gram, 1)))
    squares = jnp.full((8, 128), squares, f32)
    squares = squares + swap_tp(squares, 1)
    across, base_tile, squares = lax.optimization_barrier((across, base_tile, squares))
    across_partner = swap_tp(across, 1)
    squares = squares + swap_tp(squares, 2)
    scale = (inner_rate / jnp.sqrt(squares[0, :1] / entries + 1e-06))

    pieces = (out_grad, partner, across, across_partner)
    scale, base_tile = lax.optimization_barrier((scale, base_tile))
    sends = pseudo_gradient(FIRST + LATER, "pseudo_gradient", at, scale, ct, pieces, drift)
    waves, later = sends[:4], sends[4:]
    here, there = pass_on(waves[:2], later[:3], "x"), pass_on(waves[2:], later[3:], "y")
    there, base_tile = lax.optimization_barrier((there, base_tile))
    base_tiles = jnp.stack([base_tile, move(base_tile, "z", 1)])
    here, there = arrive(later[0], *here, "x"), arrive(later[3], *there, "y")
    here, there = lax.optimization_barrier((here, there))
    here, there = reduce_tiles(here, "y"), reduce_tiles(there, "x")
    here, there = lax.reduce_precision(here, 8, 7), lax.reduce_precision(there, 8, 7)
    crossed = move(jnp.stack([there, here]).astype(bf16), "z", 1)
    means = (jnp.stack([here, there]) + crossed.astype(f32)) / lax.axis_size("worker")
    fresh = (base_tiles - (outer_rate * (1.0 + outer_mu)) * means).astype(bf16)
    mean, tile, opposite = means[0], fresh[0], fresh[1]

    def mean_rows(k):
        return lax.dynamic_slice_in_dim(mean, ((x + k) % NX) * own_rows, own_rows, 0)

    there_got = ring(
        [jnp.concatenate([opposite, mean_rows(NX - k).astype(bf16)]) for k in (1, 2, 3)], "x", -1
    )
    here_got = ring([tile] * 3, "y", -1)
    means = jnp.stack([mean_rows(0)] + [got[TILE_R:].astype(f32) for got in there_got])
    there_got = [got[:TILE_R] for got in there_got]
    here = jnp.stack([tile] + here_got)
    there = jnp.stack([opposite] + there_got)
    here_1, here_3 = move(here, "x", -1), move(here, "x", 1)
    there_1, there_3 = move(there, "y", -1), move(there, "y", 1)
    new_master, new_momentum = outer_rows(at, master, momentum, means)
    here_1, new_master, new_momentum = lax.optimization_barrier((here_1, new_master, new_momentum))
    last = [
        move(here_1[:2], "x", -1), move(here_3[2:], "x", 1),
        move(there_1[:2], "y", -1), move(there_3[2:], "y", 1),
    ]
    rows, width = drift.shape[1], drift.shape[2]
    so_far = place(
        "place_first",
        [[(0, n, k) for n in range(4)] for k in (0, 1, 3)] + [[(1, ky, n) for n in range(4)] for ky in (0, 1, 3)],
        at, [here, here_1, here_3, there, there_1, there_3], rows, width,
    )
    new_params = place(
        "place_last",
        [[(0, 0, 2), (0, 1, 2)], [(0, 2, 2), (0, 3, 2)], [(1, 2, 0), (1, 2, 1)], [(1, 2, 2), (1, 2, 3)]],
        at, last, rows, width, so_far,
    )
    return (new_params, new_master, new_momentum)


def solution(mesh):
    placed = (
        P("worker", "tp"),
        P("worker", "tp"),
        P("worker", "tp"),
        P("worker", "tp"),
        P("worker"),
        P("worker", "tp", None),
        P(("tp", "worker"), None),
        P(("tp", "worker"), None),
    )
    return jax.shard_map(
        per_device,
        mesh=mesh,
        in_specs=placed,
        out_specs=(P("tp", None), P(("tp", "worker"), None), P(("tp", "worker"), None)),
        check_vma=False,
    )
```

```python
import functools
import math

import jax
import jax.numpy as jnp
from jax import lax
from jax.experimental import pallas as pl
from jax.experimental.pallas import tpu as pltpu
from jax.sharding import PartitionSpec as P

HD = 128
NX, NY, NZ = 4, 4, 2
TILE_R = 80
HALF_C = 640

inner_rate = 0.8
outer_rate = 0.7
outer_mu = 0.9
neg_big = -1e30
bf16 = jnp.bfloat16
f32 = jnp.float32
VMEM_LIMIT = 60 << 20


def worker_of(zh, y, x):
    return (zh % NZ) * NX * NY + (y % NY) * NX + (x % NX)


def move(value, axis, step):
    pairs = []
    for zh in range(NZ):
        for y in range(NY):
            for x in range(NX):
                to = {
                    "x": worker_of(zh, y, x + step),
                    "y": worker_of(zh, y + step, x),
                    "z": worker_of(zh + step, y, x),
                }[axis]
                pairs.append((worker_of(zh, y, x), to))
    return lax.ppermute(value, "worker", pairs)


def swap_tp(value, bit):
    return lax.ppermute(value, "tp", [(t, t ^ bit) for t in range(4)])


LOWER = [(i, j) for i in range(3) for j in range(i + 1)]


def cotangent_gram_body(grad_ref, gram_ref):
    for n, (i, j) in enumerate(LOWER):
        gram_ref[n] = lax.dot_general(
            grad_ref[i * HD:(i + 1) * HD, :], grad_ref[j * HD:(j + 1) * HD, :],
            (((1,), (1,)), ((), ())), preferred_element_type=f32,
        )


def cotangent_gram(grad):
    return pl.pallas_call(
        cotangent_gram_body,
        out_shape=jax.ShapeDtypeStruct((len(LOWER), HD, HD), f32),
        name="cotangent_gram",
    )(grad)


def attention_body(q_ref, k_ref, v_ref, seg_row_ref, ct_ref, gram_ref):
    tokens, width = q_ref.shape
    scale = 1.0 / math.sqrt(HD)
    blocks = tokens // HD
    seg_row = seg_row_ref[...]
    seg_col = jnp.broadcast_to(seg_row.astype(f32), (HD, tokens)).T.astype(jnp.int32)
    for h in range(width // HD):
        cols = slice(h * HD, (h + 1) * HD)
        for b in range(blocks):
            queries = slice(b * HD, (b + 1) * HD)
            seen = (b + 1) * HD
            scores = lax.dot_general(
                k_ref[:seen, cols], q_ref[queries, cols], (((1,), (1,)), ((), ())),
                preferred_element_type=f32,
            ) * scale
            key_at = lax.broadcasted_iota(jnp.int32, (seen, HD), 0)
            query_at = lax.broadcasted_iota(jnp.int32, (seen, HD), 1) + b * HD
            allowed = (key_at <= query_at) & (seg_col[:seen, :] == seg_row[:, queries])
            scores = jnp.where(allowed, scores, neg_big)
            exp_scores = jnp.exp(scores - jnp.max(scores, axis=0, keepdims=True))
            total = jnp.sum(exp_scores, axis=0, keepdims=True)
            weights = (exp_scores * (1.0 / total)).astype(bf16)
            ct_ref[cols, queries] = lax.dot_general(
                v_ref[:seen, cols], weights, (((0,), (0,)), ((), ())),
                preferred_element_type=f32,
            ).astype(bf16)
    for n, (i, j) in enumerate(LOWER):
        block = lax.dot_general(
            ct_ref[:, i * HD:(i + 1) * HD], ct_ref[:, j * HD:(j + 1) * HD],
            (((0,), (0,)), ((), ())), preferred_element_type=f32,
        )
        gram_ref[n] = block if i == j else 2.0 * block


def attention(queries, keys, values, segments):
    tokens, width = queries.shape
    return pl.pallas_call(
        attention_body,
        out_shape=(
            jax.ShapeDtypeStruct((width, tokens), bf16),
            jax.ShapeDtypeStruct((len(LOWER), HD, HD), f32),
        ),
        compiler_params=pltpu.CompilerParams(vmem_limit_bytes=VMEM_LIMIT),
        name="attention",
    )(queries, keys, values, segments.reshape(1, tokens))


def column_of(tp, half, quarter):
    first = (tp ^ (2 * half) ^ (quarter // 2)) * (2 * HALF_C) + (quarter % 2) * HALF_C
    return pl.multiple_of(first, HALF_C)


def row_of(zh, y, j, ky):
    return pl.multiple_of((zh ^ j) * (NY * TILE_R) + ((y + ky) % NY) * TILE_R, TILE_R)


K_ORDER = (2, 1, 3, 0)
UP_DOWN = ((2, 2, 1, 1), (3, 3, 2, 2))
FIRST = [[(0, n, far[n]) for n in range(4)] for far in UP_DOWN] + [
    [(1, far[n], n) for n in range(4)] for far in UP_DOWN
]
LATER = [
    [(0, n, 0) for n in range(4)], [(0, 0, 1), (0, 1, 1)], [(0, 2, 3), (0, 3, 3)],
    [(1, 0, n) for n in range(4)], [(1, 1, 0), (1, 1, 1)], [(1, 3, 2), (1, 3, 3)],
]


def pseudo_body(outputs, entries, at_ref, near_ref, far_ref, ct_ref, g0_ref, g1_ref, g2_ref, g3_ref, drift_ref, *rest):
    outs = rest[:len(outputs)]
    drift_buf, g_buf, rows_buf, out_buf, drift_sems, g_sems, out_sems = rest[len(outputs):]
    x, y, zh, tp = at_ref[0], at_ref[1], at_ref[2], at_ref[3]
    squares = near_ref[:1, :1] + far_ref[:1, :1]
    scale = inner_rate / jnp.sqrt(squares / entries + 1e-06)
    pieces = ((g0_ref, g1_ref), (g2_ref, g3_ref))

    def g_copy(slot, ref, k):
        return pltpu.make_async_copy(
            ref.at[:, pl.ds(pl.multiple_of(((x + k) % 2) * HALF_C, HALF_C), HALF_C)],
            g_buf.at[slot], g_sems.at[slot],
        )

    def g_start(slot, ref, k):
        g_copy(slot, ref, k).start()

    def drift_copy(slot, k, half):
        return pltpu.make_async_copy(
            drift_ref.at[0, :, pl.ds(column_of(tp, half, (x + k) % NX), HALF_C)],
            drift_buf.at[slot], drift_sems.at[slot],
        )

    steps = [(k, half) for k in K_ORDER for half in range(2)]
    for slot, (k, half) in enumerate(steps):
        for side, ref in enumerate(pieces[half]):
            pl.when(((x + k) % NX) // 2 == side)(functools.partial(g_start, slot, ref, k))
        drift_copy(slot, k, half).start()
    for j in range(2):
        for ky in range(NY):
            first = (j * NY + ky) * TILE_R
            rows_buf[first:first + TILE_R, :] = ct_ref[pl.ds(row_of(zh, y, j, ky), TILE_R), :]

    copies = []
    for slot, (k, half) in enumerate(steps):
        cols = slice(half * HALF_C, (half + 1) * HALF_C)
        g_copy(slot, g0_ref, k).wait()
        drift_copy(slot, k, half).wait()
        for j in range(2):
            rows = slice(j * NY * TILE_R, (j + 1) * NY * TILE_R)
            block = jnp.dot(rows_buf[rows, :], g_buf[slot], preferred_element_type=f32)
            for ky in range(NY):
                own = drift_buf[slot, pl.ds(row_of(zh, y, j, ky), TILE_R), :]
                value = block[ky * TILE_R:(ky + 1) * TILE_R] * scale + own.astype(f32)
                out_buf[k, j * NY + ky, :, cols] = value.astype(bf16)
        if half == 1:
            for j in range(2):
                for ky in range(NY):
                    o, index = next(
                        (o, tiles.index((j, ky, k))) for o, tiles in enumerate(outputs) if (j, ky, k) in tiles
                    )
                    copies.append(pltpu.make_async_copy(
                        out_buf.at[k, j * NY + ky], outs[o].at[index], out_sems.at[len(copies)]
                    ))
                    copies[-1].start()
    for one in copies:
        one.wait()


def pseudo_gradient(outputs, name, entries, at, squares, ct, pieces, drift):
    smem = pl.BlockSpec(memory_space=pltpu.SMEM)
    hbm = pl.BlockSpec(memory_space=pl.ANY)
    tokens, rows = ct.shape[1], ct.shape[0]
    count = sum(len(tiles) for tiles in outputs)
    return pl.pallas_call(
        functools.partial(pseudo_body, outputs, entries),
        out_shape=tuple(
            jax.ShapeDtypeStruct((len(tiles), TILE_R, 2 * HALF_C), bf16) for tiles in outputs
        ),
        in_specs=[smem] + [pl.BlockSpec(memory_space=pltpu.VMEM)] * 3 + [hbm] * 5,
        out_specs=(hbm,) * len(outputs),
        scratch_shapes=[
            pltpu.VMEM((8, rows, HALF_C), bf16),
            pltpu.VMEM((8, tokens, HALF_C), bf16),
            pltpu.VMEM(ct.shape, bf16),
            pltpu.VMEM((NX, 2 * NY, TILE_R, 2 * HALF_C), bf16),
            pltpu.SemaphoreType.DMA((8,)),
            pltpu.SemaphoreType.DMA((8,)),
            pltpu.SemaphoreType.DMA((count,)),
        ],
        compiler_params=pltpu.CompilerParams(vmem_limit_bytes=VMEM_LIMIT),
        cost_estimate=pl.CostEstimate(
            flops=2 * rows * tokens * 5120, bytes_accessed=18_000_000, transcendentals=0
        ),
        name=name,
    )(at, *squares, ct, *pieces, drift)


def base_body(at_ref, master_ref, momentum_ref, base_ref):
    tp = at_ref[3]
    for quarter in range(NX):
        for half in range(2):
            cols = pl.ds(column_of(tp, half, quarter), HALF_C)
            base_ref[quarter, :, half * HALF_C:(half + 1) * HALF_C] = (
                master_ref[:, cols] - (outer_rate * outer_mu * outer_mu) * momentum_ref[:, cols]
            )


def base_rows(at, master, momentum):
    vmem = pl.BlockSpec(memory_space=pltpu.VMEM)
    return pl.pallas_call(
        base_body,
        out_shape=jax.ShapeDtypeStruct((NX, master.shape[0], 2 * HALF_C), f32),
        in_specs=[pl.BlockSpec(memory_space=pltpu.SMEM), vmem, vmem],
        out_specs=vmem,
        name="base_rows",
    )(at, master, momentum)


def outer_body(at_ref, master_ref, momentum_ref, mean_ref, new_master_ref, new_momentum_ref):
    x, tp = at_ref[0], at_ref[3]
    for quarter in range(NX):
        for half in range(2):
            cols = pl.ds(column_of(tp, half, quarter), HALF_C)
            mean = mean_ref[(quarter - x + NX) % NX, :, half * HALF_C:(half + 1) * HALF_C]
            new = outer_mu * momentum_ref[:, cols] + mean
            new_momentum_ref[:, cols] = new
            new_master_ref[:, cols] = master_ref[:, cols] - outer_rate * (mean + outer_mu * new)


def outer_rows(at, master, momentum, mean):
    vmem = pl.BlockSpec(memory_space=pltpu.VMEM)
    out = jax.ShapeDtypeStruct(master.shape, f32)
    return pl.pallas_call(
        outer_body,
        out_shape=(out, out),
        in_specs=[pl.BlockSpec(memory_space=pltpu.SMEM), vmem, vmem, vmem],
        out_specs=(vmem, vmem),
        name="outer_rows",
    )(at, master, momentum, mean)


def place_body(where, at_ref, *rest):
    count = len(where)
    blocks, (out_ref, stage, in_sems, out_sems) = rest[:count], rest[-4:]
    x, y, zh, tp = at_ref[0], at_ref[1], at_ref[2], at_ref[3]
    slots = [sum(len(tiles) for tiles in where[:n]) for n in range(count)]
    loads = [
        pltpu.make_async_copy(blocks[n], stage.at[slots[n]:slots[n] + len(where[n])], in_sems.at[n])
        for n in range(count)
    ]
    for one in loads:
        one.start()
    stores = []
    for n, tiles in enumerate(where):
        loads[n].wait()
        for m, (j, ky, k) in enumerate(tiles):
            for half in range(2):
                stores.append(pltpu.make_async_copy(
                    stage.at[slots[n] + m, :, half * HALF_C:(half + 1) * HALF_C],
                    out_ref.at[pl.ds(row_of(zh, y, j, ky), TILE_R),
                               pl.ds(column_of(tp, half, (x + k) % NX), HALF_C)],
                    out_sems.at[len(stores)],
                ))
                stores[-1].start()
    for one in stores:
        one.wait()


def place(name, where, at, blocks, rows, width, so_far=None):
    hbm = pl.BlockSpec(memory_space=pl.ANY)
    count = sum(len(tiles) for tiles in where)
    operands = [at, *blocks] + ([] if so_far is None else [so_far])
    return pl.pallas_call(
        functools.partial(place_body, where),
        out_shape=jax.ShapeDtypeStruct((rows, width), bf16),
        in_specs=[pl.BlockSpec(memory_space=pltpu.SMEM)] + [hbm] * (len(operands) - 1),
        out_specs=hbm,
        scratch_shapes=[
            pltpu.VMEM((count, TILE_R, 2 * HALF_C), bf16),
            pltpu.SemaphoreType.DMA((len(where),)),
            pltpu.SemaphoreType.DMA((2 * count,)),
        ],
        input_output_aliases={} if so_far is None else {len(operands) - 1: 0},
        compiler_params=pltpu.CompilerParams(vmem_limit_bytes=VMEM_LIMIT),
        cost_estimate=pl.CostEstimate(
            flops=0, bytes_accessed=4 * count * TILE_R * 2 * HALF_C, transcendentals=0
        ),
        name=name,
    )(*operands)


def add(*terms):
    total = terms[0].astype(f32)
    for term in terms[1:]:
        total = total + term.astype(f32)
    return total


def ring(values, axis, sign):
    two = move(values[1], axis, 2 * sign)
    one = move(values[0], axis, sign)
    three = move(values[2], axis, -sign)
    return [one, two, three]


def pass_on(waves, later, axis):
    up, down = move(waves[0], axis, 1), move(waves[1], axis, -1)
    onward_up = add(later[1], up[:2]).astype(bf16)
    onward_down = add(later[2], down[2:]).astype(bf16)
    return up, down, onward_up, onward_down


def arrive(own, up, down, onward_up, onward_down, axis):
    last_up, last_down = move(onward_up, axis, 1), move(onward_down, axis, -1)
    low = add(own[:2], down[:2], last_up)
    high = add(own[2:], up[2:], last_down)
    return jnp.concatenate([low, high])


def reduce_tiles(tiles, axis):
    sent = tiles.astype(bf16)
    return add(tiles[0], *ring([sent[1], sent[2], sent[3]], axis, 1))


def per_device(queries, keys, values, out_grad, segments, drift, master, momentum):
    tp = lax.axis_index("tp")
    worker = lax.axis_index("worker")
    x, y, zh = worker % NX, (worker // NX) % NY, worker // (NX * NY)
    at = jnp.stack([x, y, zh, tp]).astype(jnp.int32)
    own_rows = master.shape[0]
    entries = queries.shape[1] * lax.axis_size("tp") * drift.shape[2]

    partner = swap_tp(out_grad, 1)

    gram = cotangent_gram(out_grad)
    far = swap_tp(gram, 2)

    gram, queries = lax.optimization_barrier((gram, queries))
    ct, own_gram = attention(queries, keys, values, segments)
    ct, early_at, crossing = lax.optimization_barrier((ct, at, out_grad))
    across = swap_tp(crossing, 2)
    base = base_rows(early_at, master, momentum)
    rings = [[first + n for n in range(NX)] for first in range(0, NX * NY * NZ, NX)]
    base_tile = lax.all_to_all(base, "worker", 0, 0, axis_index_groups=rings)
    base_tile = base_tile.reshape(TILE_R, 2 * HALF_C)
    far, gram, ct, own_gram = lax.optimization_barrier((far, gram, ct, own_gram))
    gram = gram + far
    squares = jnp.sum(own_gram * (gram + swap_tp(gram, 1)))
    squares = jnp.full((8, 128), squares, f32)
    squares = squares + swap_tp(squares, 1)
    across, base_tile, squares = lax.optimization_barrier((across, base_tile, squares))
    across_partner = swap_tp(across, 1)
    squares = (squares, swap_tp(squares, 2))

    pieces = (out_grad, partner, across, across_partner)
    squares, base_tile = lax.optimization_barrier((squares, base_tile))
    sends = pseudo_gradient(FIRST + LATER, "pseudo_gradient", entries, at, squares, ct, pieces, drift)
    waves, later = sends[:4], sends[4:]
    here, there = pass_on(waves[:2], later[:3], "x"), pass_on(waves[2:], later[3:], "y")
    there, base_tile = lax.optimization_barrier((there, base_tile))
    base_tiles = jnp.stack([base_tile, move(base_tile, "z", 1)])
    here, there = arrive(later[0], *here, "x"), arrive(later[3], *there, "y")
    here, there = lax.optimization_barrier((here, there))
    here, there = reduce_tiles(here, "y"), reduce_tiles(there, "x")
    here, there = lax.reduce_precision(here, 8, 7), lax.reduce_precision(there, 8, 7)
    crossed = move(jnp.stack([there, here]).astype(bf16), "z", 1)
    means = (jnp.stack([here, there]) + crossed.astype(f32)) / lax.axis_size("worker")
    fresh = (base_tiles - (outer_rate * (1.0 + outer_mu)) * means).astype(bf16)
    mean, tile, opposite = means[0], fresh[0], fresh[1]

    def mean_rows(k):
        return lax.dynamic_slice_in_dim(mean, ((x + k) % NX) * own_rows, own_rows, 0)

    there_got = ring(
        [jnp.concatenate([opposite, mean_rows(NX - k).astype(bf16)]) for k in (1, 2, 3)], "x", -1
    )
    here_got = ring([tile] * 3, "y", -1)
    means = jnp.stack([mean_rows(0)] + [got[TILE_R:].astype(f32) for got in there_got])
    there_got = [got[:TILE_R] for got in there_got]
    here = jnp.stack([tile] + here_got)
    there = jnp.stack([opposite] + there_got)
    here_1, here_3 = move(here, "x", -1), move(here, "x", 1)
    there_1, there_3 = move(there, "y", -1), move(there, "y", 1)
    new_master, new_momentum = outer_rows(at, master, momentum, means)
    here_1, new_master, new_momentum = lax.optimization_barrier((here_1, new_master, new_momentum))
    last = [
        move(here_1[:2], "x", -1), move(here_3[2:], "x", 1),
        move(there_1[:2], "y", -1), move(there_3[2:], "y", 1),
    ]
    rows, width = drift.shape[1], drift.shape[2]
    so_far = place(
        "place_first",
        [[(0, n, k) for n in range(4)] for k in (0, 1, 3)] + [[(1, ky, n) for n in range(4)] for ky in (0, 1, 3)],
        at, [here, here_1, here_3, there, there_1, there_3], rows, width,
    )
    new_params = place(
        "place_last",
        [[(0, 0, 2), (0, 1, 2)], [(0, 2, 2), (0, 3, 2)], [(1, 2, 0), (1, 2, 1)], [(1, 2, 2), (1, 2, 3)]],
        at, last, rows, width, so_far,
    )
    return (new_params, new_master, new_momentum)


def solution(mesh):
    placed = (
        P("worker", "tp"),
        P("worker", "tp"),
        P("worker", "tp"),
        P("worker", "tp"),
        P("worker"),
        P("worker", "tp", None),
        P(("tp", "worker"), None),
        P(("tp", "worker"), None),
    )
    return jax.shard_map(
        per_device,
        mesh=mesh,
        in_specs=placed,
        out_specs=(P("tp", None), P(("tp", "worker"), None), P(("tp", "worker"), None)),
        check_vma=False,
    )
```
